128 devices in a mesh: grp: 8 (over x, core), row: 16 (over z, y).
Axes of the slice: x: 4, y: 4, z: 4, core: 2. Of those that a mesh axis runs over, the one named last changes fastest.
Arguments:
- pair_feats: bfloat16 [32, 6, 128, 128, 128], P('grp', None, 'row'), may hold values from -6 to 6
- block_cols: int32 [32, 6], replicated, may hold values from 0 to 31, as said below
- attn_mask: int32 [32, 6], replicated, may hold values from 0 to 1, as said below
- chain_of_row: int32 [32], replicated, may hold values from 0 to 3
- same_chain: float32 [16], replicated, may hold values from -2 to 2
- node_feats: bfloat16 [4096, 768], P('grp'), may hold values from -6 to 6
- node_cotangent: bfloat16 [4096, 768], P('grp'), may hold values from -6 to 6
- tri_weight: bfloat16 [128, 256], replicated, may hold values from -0.5 to 0.5
- gate_weight: bfloat16 [128, 128], replicated, may hold values from -0.5 to 0.5
- tri_out_weight: bfloat16 [64, 128], replicated, may hold values from -0.75 to 0.75
- bias_weight: bfloat16 [128, 16], replicated, may hold values from -0.5 to 0.5
- query_weight: bfloat16 [768, 768], P(None, 'row'), may hold values from -8 to 8
- key_weight: bfloat16 [768, 768], P(None, 'row'), may hold values from -8 to 8
- value_weight: bfloat16 [768, 768], P(None, 'row'), may hold values from -0.21875 to 0.21875
- out_weight: bfloat16 [768, 768], P('row'), may hold values from -0.21875 to 0.21875
Outputs:
- pair_out: bfloat16 [32, 6, 128, 128, 128], P('grp', None, 'row')
- node_out: bfloat16 [4096, 768], P(('grp', 'row'))
- pair_grad: bfloat16 [32, 6, 128, 128, 128], P('grp', None, 'row')
The draws below stay inside these ranges and needn't reach their ends.
Inputs may be any that keep to these rules, and one draw needn't show every extreme that they name: `block_cols`: block row I belongs to chain group I // 4. Its 6 columns are distinct: itself in slot 0, the other block rows of its own group, and 2 block rows of other groups. The rows of one group name block rows of at most 4 other groups and at most 2 distinct block rows of any one other group; some pair of groups reaches 2. `attn_mask`: slot 0 of every block row is 1.
All inputs are finite; a program needn't handle non-finite values.
Results may differ from the reference program's by a relative error of at most 0.025.
Values may be sent and summed in bfloat16 or wider, within the bound.
A program may use at most 192 MiB of HBM per device.

```python
import jax
import jax.numpy as jnp
from jax import lax

BLK = 128
CZ = 128
CH = 64
DN = 768
HEADS = 16
HD = 48
BR_GRP = 4
KS = 6
CAPX = 2
GROUPS = 8
PARTNERS = 4
NBR = 32
NRES = 4096


def permutations(subkey, how_many, length):
    subkeys = jax.random.split(subkey, how_many)
    return jax.vmap(lambda single: jax.random.permutation(single, length))(subkeys)


def draw_block_cols(key, part):
    branches = jax.random.split(jax.random.fold_in(key, 101), 4)
    groups = jnp.arange(GROUPS, dtype=jnp.int32)
    inner_rows = jnp.arange(BR_GRP, dtype=jnp.int32)
    local_order = (inner_rows[:, None] + inner_rows[None, :]) % BR_GRP
    own_rows = groups[:, None, None] * BR_GRP + local_order[None, :, :]
    offsets = permutations(branches[0], GROUPS, GROUPS - 1)[:, :PARTNERS].astype(jnp.int32) + 1
    partner = (groups[:, None] + offsets) % GROUPS
    picked_rows = permutations(branches[1], GROUPS * PARTNERS, BR_GRP)[:, :CAPX].astype(jnp.int32)
    union_rows = (partner.reshape(GROUPS * PARTNERS, 1) * BR_GRP + picked_rows).reshape(GROUPS, PARTNERS * CAPX)
    pick_order = permutations(branches[2], GROUPS * BR_GRP, PARTNERS * CAPX).astype(jnp.int32)
    pick_order = pick_order.reshape(GROUPS, BR_GRP, PARTNERS * CAPX)
    pick_order = pick_order.at[:, 0, :].set(jnp.arange(PARTNERS * CAPX, dtype=jnp.int32))
    spread_union = jnp.broadcast_to(union_rows[:, None, :], (GROUPS, BR_GRP, PARTNERS * CAPX))
    interface = jnp.take_along_axis(spread_union, pick_order, axis=2)[:, :, :KS - BR_GRP]
    listed = jnp.concatenate([own_rows, interface], axis=2)
    tail_slots = permutations(branches[3], GROUPS * BR_GRP, KS - 1).astype(jnp.int32).reshape(GROUPS, BR_GRP, KS - 1) + 1
    shuffle = jnp.concatenate([jnp.zeros((GROUPS, BR_GRP, 1), jnp.int32), tail_slots], axis=2)
    return jnp.take_along_axis(listed, shuffle, axis=2).reshape(NBR, KS).astype(jnp.int32)


def draw_attn_mask(key, part):
    levels = jax.random.randint(jax.random.fold_in(key, 202), (NBR, KS), 0, 4)
    allowed = (levels > 0).astype(jnp.int32)
    return allowed.at[:, 0].set(1)


def draw_node_feats(key, part):
    branch = jax.random.fold_in(key, 303)
    values = jax.random.normal(jax.random.fold_in(branch, 1), (NRES, DN), jnp.float32)
    return jnp.clip(values, -6.0, 6.0).astype(jnp.bfloat16)


def query_key(key):
    branch = jax.random.fold_in(key, 404)
    query_part = jax.random.normal(jax.random.fold_in(branch, 1), (DN, DN), jnp.float32) * DN ** (-0.5)
    key_part = jax.random.normal(jax.random.fold_in(branch, 2), (DN, DN), jnp.float32) * DN ** (-0.5)
    return (query_part, key_part)


def draw_query_weight(key, part):
    query_part, key_part = query_key(key)
    return jnp.clip(query_part, -8.0, 8.0).astype(jnp.bfloat16)


def draw_key_weight(key, part):
    return jnp.clip(query_key(key)[1], -8.0, 8.0).astype(jnp.bfloat16)


def touch_ends(entries, stream_key, low, top_value):
    index_at = [jax.random.randint(jax.random.fold_in(stream_key, axis), (), 0, length) for axis, length in enumerate(entries.shape)]
    longest = entries.shape.index(max(entries.shape))
    next_to = index_at[:longest] + [(index_at[longest] + 1) % entries.shape[longest]] + index_at[longest + 1:]
    return entries.at[tuple(index_at)].set(low).at[tuple(next_to)].set(top_value)


def block_levels(stream_key, shape, shards, least, high):
    factor_of, own = 1.0, jax.random.fold_in(stream_key, 6)
    for dim, shards_of in shards:
        heights = jnp.exp(jax.random.uniform(jax.random.fold_in(own, dim), (shards_of,), jnp.float32, least / len(shards), high / len(shards)))
        factor_of = factor_of * jnp.repeat(heights, shape[dim] // shards_of).reshape([-1 if axis == dim else 1 for axis in range(len(shape))])
    return factor_of


def bell_draw(own_key, shape, scale, bound, cuts=(), held_as=jnp.bfloat16):
    array = scale * jax.random.normal(own_key, shape, jnp.float32)
    if cuts:
        array = array * block_levels(own_key, shape, cuts, -0.22, 0.18)
    return jnp.clip(array, -bound, bound).astype(held_as)


def setup_inputs(seed: int = 0) -> dict:
    key_of = jax.random.split(jax.random.key(seed), 16)
    return {
        "pair_feats": bell_draw(key_of[0], (NBR, KS, BLK, BLK, CZ), 1.0, 6.0, ((0, 8), (2, 16))),
        "block_cols": draw_block_cols(jax.random.fold_in(key_of[15], 71), 0),
        "attn_mask": draw_attn_mask(jax.random.fold_in(key_of[15], 71), 0),
        "chain_of_row": touch_ends(jax.random.randint(key_of[3], (NBR,), 0, 4), jax.random.fold_in(key_of[3], 1), 0, 3).astype(jnp.int32),
        "same_chain": jnp.clip(jax.random.uniform(key_of[4], (HEADS,), jnp.float32, -2.0, 2.0), -2.0, 2.0),
        "node_feats": draw_node_feats(jax.random.fold_in(key_of[15], 71), 0),
        "node_cotangent": bell_draw(key_of[6], (NRES, DN), 1.0, 6.0, ((0, 8),)),
        "tri_weight": bell_draw(key_of[7], (CZ, 4 * CH), CZ ** -0.5, 0.5),
        "gate_weight": bell_draw(key_of[8], (CZ, CZ), CZ ** -0.5, 0.5),
        "tri_out_weight": bell_draw(key_of[9], (CH, CZ), CH ** -0.5, 0.75),
        "bias_weight": bell_draw(key_of[10], (CZ, HEADS), CZ ** -0.5, 0.5),
        "query_weight": draw_query_weight(jax.random.fold_in(key_of[15], 71), 0),
        "key_weight": draw_key_weight(jax.random.fold_in(key_of[15], 71), 0),
        "value_weight": bell_draw(key_of[13], (DN, DN), DN ** -0.5, 0.21875, ((1, 16),)),
        "out_weight": bell_draw(key_of[14], (DN, DN), DN ** -0.5, 0.21875, ((0, 16),)),
    }


epsilon = 1e-05

def rounded(values):
    return lax.optimization_barrier(values.astype(jnp.bfloat16))

def norm_parts(values, dimension):
    center = lax.optimization_barrier(jnp.mean(values, axis=dimension, keepdims=True))
    shifted = values - center
    spread = lax.optimization_barrier(jnp.mean(shifted * shifted, axis=dimension, keepdims=True))
    inverse = lax.rsqrt(spread + epsilon)
    return (shifted * inverse, inverse)

def reference(pair_feats, block_cols, attn_mask, chain_of_row, same_chain, node_feats, node_cotangent, tri_weight, gate_weight, tri_out_weight, bias_weight, query_weight, key_weight, value_weight, out_weight):
    tri_float = tri_weight.astype(jnp.float32)
    gate_float = gate_weight.astype(jnp.float32)
    tri_out_float = tri_out_weight.astype(jnp.float32)
    bias_float = bias_weight.astype(jnp.float32)

    def project_row(pair_row):
        normed = rounded(norm_parts(pair_row.astype(jnp.float32), 3)[0]).astype(jnp.float32)
        projected = jnp.einsum('sijc,cx->sxij', normed, tri_float)
        left_proj = rounded(jax.nn.sigmoid(projected[:, CH:2 * CH]) * projected[:, :CH])
        right_proj = rounded(jax.nn.sigmoid(projected[:, 3 * CH:]) * projected[:, 2 * CH:3 * CH])
        bias_rows = rounded(jnp.einsum('sijc,ch->shij', normed, bias_float))
        return (left_proj, right_proj, bias_rows)
    left_all, right_all, bias_all = lax.map(project_row, pair_feats)

    def triangle_row(position):
        left_row = left_all[position].astype(jnp.float32)
        row_cols = block_cols[position]

        def one_slot(column):
            far_row = right_all[column].astype(jnp.float32)
            matches = (row_cols[:, None] == block_cols[column][None, :]).astype(jnp.float32)
            aligned = jnp.einsum('tu,udjk->tdjk', matches, far_row)
            return rounded(jnp.einsum('tdik,tdjk->dij', left_row, aligned))
        return lax.map(one_slot, row_cols)
    tri_all = lax.map(triangle_row, jnp.arange(NBR, dtype=jnp.int32))
    node_norm = rounded(norm_parts(node_feats.astype(jnp.float32), 1)[0])
    queries = rounded(jnp.dot(node_norm, query_weight, preferred_element_type=jnp.float32)).reshape(NBR, BLK, HEADS, HD)
    keys_all = rounded(jnp.dot(node_norm, key_weight, preferred_element_type=jnp.float32)).reshape(NBR, BLK, HEADS, HD)
    values_all = rounded(jnp.dot(node_norm, value_weight, preferred_element_type=jnp.float32)).reshape(NBR, BLK, HEADS, HD)
    cot_heads = rounded(jnp.dot(node_cotangent, out_weight.T, preferred_element_type=jnp.float32)).reshape(NBR, BLK, HEADS, HD)
    score_scale = HD ** (-0.5)

    def attend_row(position):
        row_cols = block_cols[position]
        query_rows = queries[position].astype(jnp.float32)
        near_keys = keys_all[row_cols].astype(jnp.float32)
        near_values = values_all[row_cols].astype(jnp.float32)
        same_flag = (chain_of_row[row_cols] == chain_of_row[position]).astype(jnp.float32)
        scores = jnp.einsum('ihd,sjhd->shij', query_rows, near_keys) * score_scale
        scores = scores + bias_all[position].astype(jnp.float32) + same_chain[None, :, None, None] * same_flag[:, None, None, None]
        scores = jnp.where((attn_mask[position] > 0)[:, None, None, None], scores, -jnp.inf)
        row_top = lax.optimization_barrier(jnp.max(scores, axis=(0, 3), keepdims=True))
        exp_scores = jnp.exp(scores - row_top)
        probabilities = exp_scores / lax.optimization_barrier(jnp.sum(exp_scores, axis=(0, 3), keepdims=True))
        probs_low = rounded(probabilities).astype(jnp.float32)
        mixed_heads = rounded(jnp.einsum('shij,sjhd->ihd', probs_low, near_values)).reshape(BLK, DN)
        grad_probs = jnp.einsum('ihd,sjhd->shij', cot_heads[position].astype(jnp.float32), near_values)
        row_total = lax.optimization_barrier(jnp.sum(probabilities * grad_probs, axis=(0, 3), keepdims=True))
        grad_scores = rounded(probabilities * (grad_probs - row_total))
        return (mixed_heads, grad_scores)
    mixed_rows, grad_blocks = lax.map(attend_row, jnp.arange(NBR, dtype=jnp.int32))
    node_out = (node_feats.astype(jnp.float32) + jnp.dot(mixed_rows.reshape(NRES, DN), out_weight, preferred_element_type=jnp.float32)).astype(jnp.bfloat16)

    def finish_row(position):
        pair_float = pair_feats[position].astype(jnp.float32)
        normed, pair_scale = norm_parts(pair_float, 3)
        normed_short = rounded(normed).astype(jnp.float32)
        gate_values = rounded(jax.nn.sigmoid(jnp.einsum('sijc,cy->sijy', normed_short, gate_float))).astype(jnp.float32)
        tri_norm = rounded(norm_parts(tri_all[position].astype(jnp.float32), 1)[0]).astype(jnp.float32)
        update = jnp.einsum('sxij,xc->sijc', tri_norm, tri_out_float)
        pair_out = (pair_float + gate_values * update).astype(jnp.bfloat16)
        grad_normed = jnp.einsum('shij,ch->sijc', grad_blocks[position].astype(jnp.float32), bias_float)
        centre_grad = grad_normed - lax.optimization_barrier(jnp.mean(grad_normed, axis=3, keepdims=True))
        projection_mean = lax.optimization_barrier(jnp.mean(grad_normed * normed, axis=3, keepdims=True))
        pair_grad = (pair_scale * (centre_grad - normed * projection_mean)).astype(jnp.bfloat16)
        return (pair_out, pair_grad)
    pair_out, pair_grad = lax.map(finish_row, jnp.arange(NBR, dtype=jnp.int32))
    return (pair_out, node_out, pair_grad)
```

```python
import jax
import jax.numpy as jnp
from jax import lax
from jax.experimental import pallas as pl
from jax.experimental.pallas import tpu as pltpu
from jax.sharding import PartitionSpec as P

F32 = jnp.float32
BF16 = jnp.bfloat16
MESH = pl.DeviceIdType.MESH
EPS = 1e-5
GRP, ROW = 8, 16
BR, KS, BLK, CZ, CH = 4, 6, 128, 128, 64
NB = BR * KS
QC = CH // ROW
PAD = 128
VOFF = 64
ROW_ORDER = (1, 3, 4, 12, 2, 8, 5, 15, 7, 13, 6, 14, 9, 11, 10)
GRP_ORDER = (2, 6, 4, 3, 7, 5, 1)


def row_peer(row, offset):
    z, y = row // 4, row % 4
    return ((z + offset // 4) % 4) * 4 + (y + offset % 4) % 4


def grp_peer(grp, offset):
    x, core = grp // 2, grp % 2
    return ((x + offset // 2) % 4) * 2 + (core + offset % 2) % 2


def layer_norm(values):
    center = jnp.mean(values, axis=-1, keepdims=True)
    shifted = values - center
    spread = jnp.mean(shifted * shifted, axis=-1, keepdims=True)
    inverse = lax.rsqrt(spread + EPS)
    return shifted * inverse, inverse


def dot_nt(a, b):
    return lax.dot_general(a, b, (((1,), (1,)), ((), ())), preferred_element_type=F32)


def dot_nn(a, b):
    return lax.dot_general(a, b, (((1,), (0,)), ((), ())), preferred_element_type=F32)


def dot_tn(a, b):
    return lax.dot_general(a, b, (((0,), (0,)), ((), ())), preferred_element_type=F32)


def i32(flag):
    return jnp.where(flag, 1, 0).astype(jnp.int32)


def named_ranks(cols, reader, owner):
    flags = [jnp.int32(0)] * BR
    for r in range(BR):
        for s in range(KS):
            c = cols[reader * BR + r, s]
            for l in range(BR):
                flags[l] = flags[l] | i32(c == owner * BR + l)
    ranks, count = [], jnp.int32(0)
    firsts = [jnp.int32(0), jnp.int32(0)]
    for l in range(BR):
        ranks.append(count)
        for a in range(2):
            firsts[a] = firsts[a] + l * flags[l] * i32(count == a)
        count = count + flags[l]
    return ranks, firsts


def pick(entries, index):
    out = jnp.int32(0)
    for n, entry in enumerate(entries):
        out = out + entry * i32(index == n)
    return out


def write_tables(cols, grp, step, place, kvplace, stage, kvstage):
    inner = step // KS
    slot = step % KS
    j = cols[grp * BR + inner, slot]
    owner = j >> 2
    own = owner == grp
    ranks, _ = named_ranks(cols, grp, owner)
    offset = ((grp // 2 - owner // 2 + 4) % 4) * 2 + (grp % 2 - owner % 2 + 2) % 2
    rank_j = pick(ranks, j & 3)
    theirs = [cols[j, u] for u in range(KS)]
    for t in range(KS):
        c = cols[grp * BR + inner, t]
        found, far, count = jnp.int32(-1), jnp.int32(0), jnp.int32(0)
        for u in range(KS):
            hit = theirs[u] == c
            found = jnp.where(hit, u, found)
            far = jnp.where(hit, count, far)
            count = count + i32((theirs[u] >> 2) != owner)
        n = jnp.where((c >> 2) == owner, pick(ranks, c & 3), 2 + far)
        remote = NB + (offset - 1) * 8 + rank_j * 4 + n
        place[step * KS + t] = jnp.where(
            found >= 0, jnp.where(own, (j & 3) * KS + found, remote), NB + 56
        )
    kvplace[step] = jnp.where(own, j & 3, BR + (offset - 1) * 2 + rank_j)
    to = 1 + step % 7
    reader = grp_peer(grp, to)
    _, firsts = named_ranks(cols, reader, grp)
    for a in range(2):
        near, far = [jnp.int32(0)] * 2, [jnp.int32(0)] * 2
        count = jnp.int32(0)
        for u in range(KS):
            c = cols[grp * BR + firsts[a], u]
            away = i32((c >> 2) != grp)
            for n in range(2):
                near[n] = near[n] + u * i32(c == grp * BR + firsts[n])
                far[n] = far[n] + u * away * i32(count == n)
            count = count + away
        for n in range(2):
            stage[(to - 1) * 8 + a * 4 + n] = firsts[a] * KS + near[n]
            stage[(to - 1) * 8 + a * 4 + 2 + n] = firsts[a] * KS + far[n]
        kvstage[(to - 1) * 2 + a] = firsts[a]


def project_kernel(
    cols, pair, tri_w, bias_w, left, right, bias, place, kvplace, stage, kvstage, weights, turned
):
    grp = lax.axis_index("grp")
    step = pl.program_id(0)

    @pl.when(step == 0)
    def _():
        weights[: 4 * CH, :] = tri_w[...].astype(F32).T.astype(BF16)
        weights[4 * CH :, :] = bias_w[...]

    write_tables(cols, grp, step, place, kvplace, stage, kvstage)
    for i in range(8):
        normed = layer_norm(pair[0, i].astype(F32))[0].astype(BF16)
        projected = dot_nt(weights[...], normed)
        turned[pl.ds(i, CH, stride=8), :] = (
            jax.nn.sigmoid(projected[CH : 2 * CH]) * projected[:CH]
        )
        turned[pl.ds(8 * CH + i, CH, stride=8), :] = (
            jax.nn.sigmoid(projected[3 * CH : 4 * CH]) * projected[2 * CH : 3 * CH]
        )
        turned[pl.ds(16 * CH + i, ROW, stride=8), :] = projected[4 * CH :]
    left[:, 0] = turned[: 8 * CH].reshape(CH, 8, BLK).astype(BF16)
    right[:, 0] = turned[8 * CH : 16 * CH].reshape(CH, 8, BLK).astype(BF16)
    bias[:, 0] = turned[16 * CH :].reshape(ROW, 8, BLK).astype(BF16)


def project(cols, pair, tri_w, bias_w):
    smem = pl.BlockSpec(memory_space=pltpu.SMEM)
    by_block = lambda n: pl.BlockSpec((n, 1, 8, BLK), lambda b: (0, b, 0, 0))
    whole = lambda a: pl.BlockSpec(a.shape, lambda b: (0,) * a.ndim)
    return pl.pallas_call(
        project_kernel,
        grid=(NB,),
        in_specs=[
            smem,
            pl.BlockSpec((1, 8, BLK, CZ), lambda b: (b, 0, 0, 0)),
            whole(tri_w),
            whole(bias_w),
        ],
        out_specs=[by_block(CH), by_block(CH), by_block(ROW), smem, smem, smem, smem],
        out_shape=[
            jax.ShapeDtypeStruct((CH, NB, 8, BLK), BF16),
            jax.ShapeDtypeStruct((CH, NB, 8, BLK), BF16),
            jax.ShapeDtypeStruct((ROW, NB, 8, BLK), BF16),
            jax.ShapeDtypeStruct((NB * KS,), jnp.int32),
            jax.ShapeDtypeStruct((NB,), jnp.int32),
            jax.ShapeDtypeStruct((56,), jnp.int32),
            jax.ShapeDtypeStruct((14,), jnp.int32),
        ],
        scratch_shapes=[
            pltpu.VMEM((4 * CH + ROW, CZ), BF16),
            pltpu.VMEM(((2 * CH + ROW) * 8, BLK), F32),
        ],
        compiler_params=pltpu.CompilerParams(vmem_limit_bytes=40 << 20),
        name="project",
    )(cols, pair, tri_w, bias_w)


def exchange_kernel(*refs):
    (
        cols, mask, chain, same, place, kvplace, stage, kvstage,
        left_in, right_in, bias_in, nodes, cotan, q_w, k_w, v_w, o_w,
        tri_out, grad_out, node_out,
    ) = refs[:20]
    scr = list(refs[20:])
    take = lambda n: [scr.pop(0) for _ in range(n)]
    right = take(QC)
    left = take(QC)
    tri = take(QC)
    xs = take(QC)
    xr = take(QC)
    (bias, grads, kv_own, kv_s, kv_r, kv_all, queries, cots, mixed, mixed_r, wo_all,
     wq_pad, wkv_pad, wo_pad, scores, gprobs) = take(16)
    (right_ss, right_rs, left_ss, left_rs, tri_ss, tri_rs, x_ss, x_rs,
     kv_ss, kv_rs, bias_ss, bias_rs, grad_ss, grad_rs, mix_ss, mix_rs, wo_ss, wo_rs, own_s) = take(19)

    grp = lax.axis_index("grp")
    row = lax.axis_index("row")
    mine = pl.ds(pl.multiple_of(row * 8, 8), 8)

    def to_row(src, dst, ss, rs, peer):
        return pltpu.make_async_remote_copy(
            src, dst, ss, rs, device_id=(grp, peer), device_id_type=MESH
        )

    def to_grp(src, dst, ss, rs, peer):
        return pltpu.make_async_remote_copy(
            src, dst, ss, rs, device_id=(peer, row), device_id_type=MESH
        )

    wo_all[...] = jnp.zeros_like(wo_all)
    wo_pad[...] = jnp.zeros_like(wo_pad)

    barrier = pltpu.get_barrier_semaphore()
    for offset in ROW_ORDER:
        pl.semaphore_signal(barrier, inc=1, device_id=(grp, row_peer(row, offset)), device_id_type=MESH)
    for offset in GRP_ORDER:
        pl.semaphore_signal(barrier, inc=1, device_id=(grp_peer(grp, offset), row), device_id_type=MESH)
    pl.semaphore_wait(barrier, 22)

    peers = [row_peer(row, offset) for offset in ROW_ORDER]

    bias_c = [
        to_row(bias_in.at[p], bias.at[:, mine, :], bias_ss.at[n], bias_rs.at[n], p)
        for n, p in enumerate(peers)
    ]
    right_c = [
        [
            to_row(right_in.at[q * ROW + p], right[q].at[:, mine, :], right_ss.at[q, n], right_rs.at[q, n], p)
            for n, p in enumerate(peers)
        ]
        for q in range(QC)
    ]
    left_c = [
        [
            to_row(left_in.at[q * ROW + p], left[q].at[:, mine, :], left_ss.at[q, n], left_rs.at[q, n], p)
            for n, p in enumerate(peers)
        ]
        for q in range(QC)
    ]
    wo_c = [
        to_row(o_w, wo_all.at[row, pl.ds(VOFF, 48), :], wo_ss.at[n], wo_rs.at[n], p)
        for n, p in enumerate(peers)
    ]
    own_c = (
        [pltpu.make_async_copy(right_in.at[q * ROW + row], right[q].at[:, mine, :], own_s.at[q]) for q in range(QC)]
        + [pltpu.make_async_copy(left_in.at[q * ROW + row], left[q].at[:, mine, :], own_s.at[QC + q]) for q in range(QC)]
        + [pltpu.make_async_copy(bias_in.at[row], bias.at[:, mine, :], own_s.at[2 * QC])]
        + [pltpu.make_async_copy(o_w, wo_all.at[row, pl.ds(VOFF, 48), :], own_s.at[2 * QC + 1])]
    )
    for c in right_c[0]:
        c.start()
    for c in own_c:
        c.start()
    for q in range(1, QC):
        for c in right_c[q]:
            c.start()
    for c in bias_c:
        c.start()
    for q in range(QC):
        for c in left_c[q]:
            c.start()
    for c in wo_c:
        c.start()

    wq_pad[...] = jnp.zeros_like(wq_pad)
    wkv_pad[...] = jnp.zeros_like(wkv_pad)
    wq_pad[:, :48] = q_w[...]
    wkv_pad[:, :48] = k_w[...]
    wkv_pad[:, VOFF : VOFF + 48] = v_w[...]
    wo_pad[VOFF : VOFF + 48, :] = o_w[...]

    @pl.loop(0, BR)
    def _(r):
        part = pl.ds(pl.multiple_of(r * BLK, BLK), BLK)
        normed = layer_norm(nodes[part, :].astype(F32))[0].astype(BF16)
        queries[r] = dot_nn(normed, wq_pad[...]).astype(BF16)
        kv_own[r] = dot_nn(normed, wkv_pad[...]).astype(BF16)
        cots[r] = dot_nt(cotan[part, :], wo_pad[...]).astype(BF16)

    for n in range(14):
        kv_s[n] = kv_own[kvstage[n]]
    gpeers = [grp_peer(grp, offset) for offset in GRP_ORDER]
    kv_c = [
        to_grp(kv_s.at[pl.ds((o - 1) * 2, 2)], kv_r.at[pl.ds((o - 1) * 2, 2)], kv_ss.at[n], kv_rs.at[n], gpeers[n])
        for n, o in enumerate(GRP_ORDER)
    ]
    for c in kv_c:
        c.start()

    x_c = []
    for q in range(QC):
        own_c[q].wait()
        for c in right_c[q]:
            c.wait()

        @pl.loop(0, 56)
        def _(n):
            xs[q][n] = right[q][stage[n]]

        x_c.append([
            to_grp(xs[q].at[pl.ds((o - 1) * 8, 8)], xr[q].at[pl.ds((o - 1) * 8, 8)], x_ss.at[q, n], x_rs.at[q, n], gpeers[n])
            for n, o in enumerate(GRP_ORDER)
        ])
        for c in x_c[q]:
            c.start()

    for c in kv_c:
        c.wait()
    own_c[2 * QC].wait()
    for c in bias_c:
        c.wait()
    kv_all[:BR] = kv_own[...]
    kv_all[BR:] = kv_r[...]
    chain_bias = same[row]

    @pl.loop(0, BR)
    def _(r):
        here = chain[grp * BR + r]
        query = queries[r]
        cot = cots[r]
        top = jnp.full((BLK, 1), -jnp.inf, F32)
        for s in range(KS):
            kv = kv_all[kvplace[r * KS + s]]
            j = cols[grp * BR + r, s]
            extra = jnp.where(chain[j] == here, chain_bias, 0.0)
            part = dot_nt(query, kv) * (48 ** -0.5) + (bias[r * KS + s].astype(F32) + extra)
            part = jnp.where(mask[grp * BR + r, s] > 0, part, -jnp.inf)
            scores[s] = part
            gprobs[s] = dot_nt(cot, kv)
            top = jnp.maximum(top, jnp.max(part, axis=1, keepdims=True))
        total = jnp.zeros((BLK, 1), F32)
        for s in range(KS):
            part = jnp.exp(scores[s] - top)
            scores[s] = part
            total = total + jnp.sum(part, axis=1, keepdims=True)
        inverse = 1.0 / total
        dots = jnp.zeros((BLK, 1), F32)
        mix = jnp.zeros((BLK, PAD), F32)
        for s in range(KS):
            probs = scores[s] * inverse
            scores[s] = probs
            dots = dots + jnp.sum(probs * gprobs[s], axis=1, keepdims=True)
            mix = mix + dot_nn(probs.astype(BF16), kv_all[kvplace[r * KS + s]])
        for s in range(KS):
            grads[r * KS + s] = (scores[s] * (gprobs[s] - dots)).astype(BF16)
        mixed[pl.ds(pl.multiple_of(r * BLK, BLK), BLK), :] = mix.astype(BF16)

    slot = lambda p: pl.ds(pl.multiple_of(p * 8, 8), 8)
    rows32 = lambda p: pl.ds(pl.multiple_of(p * 32, 32), 32)
    mix_c = [
        to_row(mixed.at[rows32(p)], mixed_r.at[row], mix_ss.at[n], mix_rs.at[n], p) for n, p in enumerate(peers)
    ]
    mix_own = pltpu.make_async_copy(mixed.at[rows32(row)], mixed_r.at[row], own_s.at[2 * QC + 2])
    grad_c = [
        to_row(grads.at[:, slot(p), :], grad_out.at[row], grad_ss.at[n], grad_rs.at[n], p)
        for n, p in enumerate(peers)
    ]
    grad_own = pltpu.make_async_copy(grads.at[:, mine, :], grad_out.at[row], own_s.at[2 * QC + 3])
    for c in mix_c + [mix_own] + grad_c + [grad_own]:
        c.start()

    tri_c, tri_own = [], []
    for q in range(QC):
        own_c[QC + q].wait()
        for c in left_c[q]:
            c.wait()
        for c in x_c[q]:
            c.wait()

        @pl.loop(0, NB)
        def _(b):
            r = b // KS
            lhs, rhs = [], []
            for t in range(KS):
                code = place[b * KS + t]
                near = right[q][jnp.minimum(code, NB - 1)]
                far = xr[q][jnp.clip(code - NB, 0, 55)]
                block = jnp.where(code < NB, near, far)
                rhs.append(jnp.where(code < NB + 56, block, jnp.zeros_like(block)))
                lhs.append(left[q][r * KS + t])
            tri[q][b] = dot_nt(jnp.concatenate(lhs, axis=1), jnp.concatenate(rhs, axis=1)).astype(BF16)

        tri_c.append([
            to_row(tri[q].at[:, slot(p), :], tri_out.at[q, row], tri_ss.at[q, n], tri_rs.at[q, n], p)
            for n, p in enumerate(peers)
        ])
        tri_own.append(pltpu.make_async_copy(tri[q].at[:, mine, :], tri_out.at[q, row], own_s.at[2 * QC + 4 + q]))
        for c in tri_c[q] + [tri_own[q]]:
            c.start()

    own_c[2 * QC + 1].wait()
    for c in wo_c + mix_c + [mix_own]:
        c.wait()
    acc = nodes[rows32(row), :].astype(F32)
    for p in range(ROW):
        acc = acc + dot_nn(mixed_r[p], wo_all[p])
    node_out[...] = acc.astype(BF16)

    for c in grad_c + [grad_own]:
        c.wait()
    for q in range(QC):
        for c in tri_c[q] + [tri_own[q]]:
            c.wait()


def exchange(scalars, tensors, nodes):
    smem = pl.BlockSpec(memory_space=pltpu.SMEM)
    vmem = pl.BlockSpec(memory_space=pltpu.VMEM)
    anyspace = pl.BlockSpec(memory_space=pl.ANY)
    dma = pltpu.SemaphoreType.DMA
    blocks = lambda n: pltpu.VMEM((n, BLK, BLK), BF16)
    n = ROW - 1
    scratch = (
        [blocks(NB)] * QC + [blocks(NB)] * QC + [blocks(NB)] * QC + [blocks(56)] * QC + [blocks(56)] * QC
        + [
            blocks(NB), blocks(NB), blocks(BR), blocks(14), blocks(14), blocks(BR + 14), blocks(BR), blocks(BR),
            pltpu.VMEM((BR * BLK, PAD), BF16), pltpu.VMEM((ROW, 32, PAD), BF16),
            pltpu.VMEM((ROW, PAD, 768), BF16), pltpu.VMEM((768, PAD), BF16), pltpu.VMEM((768, PAD), BF16),
            pltpu.VMEM((PAD, 768), BF16), pltpu.VMEM((KS, BLK, BLK), F32), pltpu.VMEM((KS, BLK, BLK), F32),
        ]
        + [dma((QC, n))] * 6 + [dma((QC, 7))] * 2 + [dma((7,))] * 2 + [dma((n,))] * 8 + [dma((2 * QC + 4 + QC,))]
    )
    return pl.pallas_call(
        exchange_kernel,
        in_specs=[smem] * 8 + [anyspace] * 3 + [vmem] * 6,
        out_specs=[anyspace, anyspace, vmem],
        out_shape=[
            jax.ShapeDtypeStruct((QC, ROW, NB, 8, BLK), BF16),
            jax.ShapeDtypeStruct((ROW, NB, 8, BLK), BF16),
            jax.ShapeDtypeStruct((32, 768), BF16),
        ],
        scratch_shapes=scratch,
        compiler_params=pltpu.CompilerParams(
            collective_id=0, has_side_effects=True, vmem_limit_bytes=63 << 20
        ),
        name="exchange",
    )(*scalars, *tensors, *nodes)


def finish_kernel(pair, tri, grads, gate_w, out_w, bias_w, pair_out, pair_grad, weights, turned):
    @pl.when(pl.program_id(0) == 0)
    def _():
        weights[...] = jnp.zeros_like(weights)
        weights[:CH, :CZ] = out_w[...]
        weights[CH:, CZ:] = bias_w[...]

    sums = tri[:, 0].astype(F32)
    shifted = sums - jnp.mean(sums, axis=0, keepdims=True)
    spread = jnp.mean(shifted * shifted, axis=0, keepdims=True)
    turned[: 8 * CH] = (shifted * lax.rsqrt(spread + EPS)).reshape(8 * CH, BLK)
    turned[8 * CH :] = grads[:, 0].astype(F32).reshape(8 * ROW, BLK)
    for i in range(8):
        hidden = turned[pl.ds(i, CH + ROW, stride=8), :].astype(BF16)
        both = dot_tn(hidden, weights[...])
        feats = pair[0, i].astype(F32)
        normed, scale = layer_norm(feats)
        gate = jax.nn.sigmoid(dot_nn(normed.astype(BF16), gate_w[...])).astype(BF16).astype(F32)
        pair_out[0, i] = (feats + gate * both[:, :CZ]).astype(BF16)
        grad = both[:, CZ:]
        centred = grad - jnp.mean(grad, axis=-1, keepdims=True)
        along = jnp.mean(grad * normed, axis=-1, keepdims=True)
        pair_grad[0, i] = (scale * (centred - normed * along)).astype(BF16)


def finish(pair, tri, grads, gate_w, out_w, bias_w):
    by_block = lambda n: pl.BlockSpec((n, 1, 8, BLK), lambda b: (0, b, 0, 0))
    whole = lambda a: pl.BlockSpec(a.shape, lambda b: (0,) * a.ndim)
    pair_spec = pl.BlockSpec((1, 8, BLK, CZ), lambda b: (b, 0, 0, 0))
    return pl.pallas_call(
        finish_kernel,
        grid=(NB,),
        in_specs=[pair_spec, by_block(CH), by_block(ROW), whole(gate_w), whole(out_w), whole(bias_w)],
        out_specs=[pair_spec, pair_spec],
        out_shape=[jax.ShapeDtypeStruct(pair.shape, BF16)] * 2,
        scratch_shapes=[
            pltpu.VMEM((CH + ROW, 2 * CZ), BF16),
            pltpu.VMEM(((CH + ROW) * 8, BLK), F32),
        ],
        compiler_params=pltpu.CompilerParams(vmem_limit_bytes=40 << 20),
        name="finish",
    )(pair, tri, grads, gate_w, out_w, bias_w)


def per_device(
    pair_feats,
    block_cols,
    attn_mask,
    chain_of_row,
    same_chain,
    node_feats,
    node_cotangent,
    tri_weight,
    gate_weight,
    tri_out_weight,
    bias_weight,
    query_weight,
    key_weight,
    value_weight,
    out_weight,
):
    pair = pair_feats.reshape(NB, 8, BLK, CZ)
    bias_t = bias_weight.T
    left, right, bias, place, kvplace, stage, kvstage = project(block_cols, pair, tri_weight, bias_t)
    tri, grads, node_out = exchange(
        (block_cols, attn_mask, chain_of_row, same_chain, place, kvplace, stage, kvstage),
        (left, right, bias),
        (node_feats, node_cotangent, query_weight, key_weight, value_weight, out_weight),
    )
    pair_out, pair_grad = finish(
        pair, tri.reshape(CH, NB, 8, BLK), grads, gate_weight, tri_out_weight, bias_t
    )
    return pair_out.reshape(pair_feats.shape), node_out, pair_grad.reshape(pair_feats.shape)


def solution(mesh):
    pair_spec = P("grp", None, "row", None, None)
    node_spec = P("grp", None)
    in_specs = (
        (pair_spec,) + (P(),) * 4 + (node_spec,) * 2 + (P(),) * 4 + (P(None, "row"),) * 3 + (P("row", None),)
    )
    out_specs = (pair_spec, P(("grp", "row"), None), pair_spec)
    return jax.shard_map(per_device, mesh=mesh, in_specs=in_specs, out_specs=out_specs, check_vma=False)
```

```python
import jax
import jax.numpy as jnp
from jax import lax
from jax.experimental import pallas as pl
from jax.experimental.pallas import tpu as pltpu
from jax.sharding import PartitionSpec as P

F32 = jnp.float32
BF16 = jnp.bfloat16
MESH = pl.DeviceIdType.MESH
EPS = 1e-5
GRP, ROW = 8, 16
BR, KS, BLK, CZ, CH = 4, 6, 128, 128, 64
NB = BR * KS
QC = CH // ROW
PAD = 128
VOFF = 64
HALVES = ((0, 6), (6, 18))
ROW_ORDER = (1, 3, 4, 12, 2, 8, 5, 15, 7, 13, 6, 14, 9, 11, 10)
GRP_ORDER = (2, 6, 4, 3, 7, 5, 1)


def row_peer(row, offset):
    z, y = row // 4, row % 4
    return ((z + offset // 4) % 4) * 4 + (y + offset % 4) % 4


def grp_peer(grp, offset):
    x, core = grp // 2, grp % 2
    return ((x + offset // 2) % 4) * 2 + (core + offset % 2) % 2


def shift_and_scale(values, ones, shifted, inverse):
    inverse[...] = dot_nn(values, ones)
    shifted[...] = values.astype(F32) - inverse[...]
    inverse[...] = dot_nn((shifted[...] * shifted[...]).astype(BF16), ones)
    inverse[...] = lax.rsqrt(inverse[...] + EPS)


def layer_norm(values):
    center = jnp.mean(values, axis=-1, keepdims=True)
    shifted = values - center
    spread = jnp.mean(shifted * shifted, axis=-1, keepdims=True)
    inverse = lax.rsqrt(spread + EPS)
    return shifted * inverse, inverse


def dot_nt(a, b):
    return lax.dot_general(a, b, (((1,), (1,)), ((), ())), preferred_element_type=F32)


def dot_nn(a, b):
    return lax.dot_general(a, b, (((1,), (0,)), ((), ())), preferred_element_type=F32)


def dot_tn(a, b):
    return lax.dot_general(a, b, (((0,), (0,)), ((), ())), preferred_element_type=F32)


def i32(flag):
    return jnp.where(flag, 1, 0).astype(jnp.int32)


def named_ranks(cols, reader, owner):
    flags = [jnp.int32(0)] * BR
    for r in range(BR):
        for s in range(KS):
            c = cols[s, reader * BR + r]
            for l in range(BR):
                flags[l] = flags[l] | i32(c == owner * BR + l)
    ranks, count = [], jnp.int32(0)
    firsts = [jnp.int32(0), jnp.int32(0)]
    for l in range(BR):
        ranks.append(count)
        for a in range(2):
            firsts[a] = firsts[a] + l * flags[l] * i32(count == a)
        count = count + flags[l]
    return ranks, firsts


def pick(entries, index):
    out = jnp.int32(0)
    for n, entry in enumerate(entries):
        out = out + entry * i32(index == n)
    return out


def write_places(cols, grp, step, place, kvplace):
    inner = step // KS
    slot = step % KS
    j = cols[slot, grp * BR + inner]
    owner = j >> 2
    own = owner == grp
    ranks, _ = named_ranks(cols, grp, owner)
    offset = ((grp // 2 - owner // 2 + 4) % 4) * 2 + (grp % 2 - owner % 2 + 2) % 2
    rank_j = pick(ranks, j & 3)
    theirs = [cols[u, j] for u in range(KS)]
    for t in range(KS):
        c = cols[t, grp * BR + inner]
        found, far, count = jnp.int32(-1), jnp.int32(0), jnp.int32(0)
        for u in range(KS):
            hit = theirs[u] == c
            found = jnp.where(hit, u, found)
            far = jnp.where(hit, count, far)
            count = count + i32((theirs[u] >> 2) != owner)
        n = jnp.where((c >> 2) == owner, pick(ranks, c & 3), 2 + far)
        remote = NB + (offset - 1) * 8 + rank_j * 4 + n
        place[step * KS + t] = jnp.where(
            found >= 0, jnp.where(own, (j & 3) * KS + found, remote), NB + 56
        )
    kvplace[step] = jnp.where(own, j & 3, BR + (offset - 1) * 2 + rank_j)


def write_stages(cols, grp, to, stage, kvstage):
    reader = grp_peer(grp, to)
    _, firsts = named_ranks(cols, reader, grp)
    for a in range(2):
        near, far = [jnp.int32(0)] * 2, [jnp.int32(0)] * 2
        count = jnp.int32(0)
        for u in range(KS):
            c = cols[u, grp * BR + firsts[a]]
            away = i32((c >> 2) != grp)
            for n in range(2):
                near[n] = near[n] + u * i32(c == grp * BR + firsts[n])
                far[n] = far[n] + u * away * i32(count == n)
            count = count + away
        for n in range(2):
            stage[(to - 1) * 8 + a * 4 + n] = firsts[a] * KS + near[n]
            stage[(to - 1) * 8 + a * 4 + 2 + n] = firsts[a] * KS + far[n]
        kvstage[(to - 1) * 2 + a] = firsts[a]


def exchange_kernel(*refs):
    (
        cols, mask, chain, same, pair, tri_w, bias_w, nodes, cotan, q_w, k_w, v_w, o_w,
        tri_out, grad_out, node_out,
    ) = refs[:16]
    scr = list(refs[16:])
    take = lambda n: [scr.pop(0) for _ in range(n)]
    right = take(QC)
    left = take(QC)
    tri = take(QC)
    xs = take(QC)
    xr = take(QC)
    sources = [take(3) for _ in range(2)]
    pair_v = take(2)
    weights, ones, turned, shifted, inverse, normed_s, place, kvplace, stage, kvstage = take(10)
    (bias, grads, kv_own, kv_s, kv_r, kv_all, queries, cots, mixed, mixed_r, wo_all,
     wq_pad, wkv_pad, wo_pad, scores, gprobs) = take(16)
    (right_ss, right_rs, left_ss, left_rs, tri_ss, tri_rs, x_ss, x_rs,
     kv_ss, kv_rs, grad_ss, grad_rs, mix_ss, mix_rs, wo_ss, wo_rs, bias_ss, bias_rs, own_s, pair_s) = take(20)

    grp = lax.axis_index("grp")
    row = lax.axis_index("row")
    mine = pl.ds(pl.multiple_of(row * 8, 8), 8)

    def to_row(src, dst, ss, rs, peer):
        return pltpu.make_async_remote_copy(
            src, dst, ss, rs, device_id=(grp, peer), device_id_type=MESH
        )

    def to_grp(src, dst, ss, rs, peer):
        return pltpu.make_async_remote_copy(
            src, dst, ss, rs, device_id=(peer, row), device_id_type=MESH
        )

    loads = [
        pltpu.make_async_copy(pair.at[pl.ds(first, count)], pair_v[h], pair_s.at[h])
        for h, (first, count) in enumerate(HALVES)
    ]
    for c in loads:
        c.start()

    wo_all[...] = jnp.zeros_like(wo_all)
    wo_pad[...] = jnp.zeros_like(wo_pad)
    weights[: 4 * CH, :] = (tri_w[...].astype(F32).T * 0.5).astype(BF16)
    weights[4 * CH :, :] = bias_w[...]
    ones[...] = jnp.full_like(ones, 1.0 / CZ)

    barrier = pltpu.get_barrier_semaphore()
    for offset in ROW_ORDER:
        pl.semaphore_signal(barrier, inc=1, device_id=(grp, row_peer(row, offset)), device_id_type=MESH)
    for offset in GRP_ORDER:
        pl.semaphore_signal(barrier, inc=1, device_id=(grp_peer(grp, offset), row), device_id_type=MESH)
    pl.semaphore_wait(barrier, 22)

    peers = [row_peer(row, offset) for offset in ROW_ORDER]

    right_c = [[] for _ in range(QC)]
    left_c = [[] for _ in range(QC)]
    bias_c = []
    own_right, own_left, own_bias = [[] for _ in range(QC)], [[] for _ in range(QC)], []
    for h, (first, count) in enumerate(HALVES):
        left_s, right_s, bias_s = sources[h]
        here = pl.ds(first, count)
        for q in range(QC):
            right_c[q].append([
                to_row(right_s.at[q * ROW + p], right[q].at[here, mine, :], right_ss.at[h * QC + q, n], right_rs.at[h * QC + q, n], p)
                for n, p in enumerate(peers)
            ])
            left_c[q].append([
                to_row(left_s.at[q * ROW + p], left[q].at[here, mine, :], left_ss.at[h * QC + q, n], left_rs.at[h * QC + q, n], p)
                for n, p in enumerate(peers)
            ])
            own_right[q].append(pltpu.make_async_copy(right_s.at[q * ROW + row], right[q].at[here, mine, :], own_s.at[h, q]))
            own_left[q].append(pltpu.make_async_copy(left_s.at[q * ROW + row], left[q].at[here, mine, :], own_s.at[h, QC + q]))
        bias_c.append([
            to_row(bias_s.at[p], bias.at[here, mine, :], bias_ss.at[h, n], bias_rs.at[h, n], p)
            for n, p in enumerate(peers)
        ])
        own_bias.append(pltpu.make_async_copy(bias_s.at[row], bias.at[here, mine, :], own_s.at[h, 2 * QC]))
    wo_c = [
        to_row(o_w, wo_all.at[row, pl.ds(VOFF, 48), :], wo_ss.at[n], wo_rs.at[n], p)
        for n, p in enumerate(peers)
    ]
    wo_own = pltpu.make_async_copy(o_w, wo_all.at[row, pl.ds(VOFF, 48), :], own_s.at[0, 2 * QC + 1])

    for h, (first, count) in enumerate(HALVES):
        left_s, right_s, bias_s = sources[h]
        loads[h].wait()

        @pl.loop(0, count)
        def _(b):
            shift_and_scale(pair_v[h][b].reshape(8 * BLK, CZ), ones[...], shifted, inverse)
            normed_s[...] = (shifted[...] * inverse[...]).astype(BF16)
            for i in range(8):
                projected = dot_nt(weights[...], normed_s[i * BLK : (i + 1) * BLK, :])
                turned[pl.ds(i, CH, stride=8), :] = (jnp.tanh(projected[CH : 2 * CH]) + 1.0) * projected[:CH]
                turned[pl.ds(8 * CH + i, CH, stride=8), :] = (
                    jnp.tanh(projected[3 * CH : 4 * CH]) + 1.0
                ) * projected[2 * CH : 3 * CH]
                turned[pl.ds(16 * CH + i, ROW, stride=8), :] = projected[4 * CH :]
            left_s[:, b] = turned[: 8 * CH].reshape(CH, 8, BLK).astype(BF16)
            right_s[:, b] = turned[8 * CH : 16 * CH].reshape(CH, 8, BLK).astype(BF16)
            bias_s[:, b] = turned[16 * CH :].reshape(ROW, 8, BLK).astype(BF16)

        for q in range(QC):
            for c in right_c[q][h] + [own_right[q][h]]:
                c.start()
        if h == 0:
            for c in bias_c[0] + [own_bias[0]]:
                c.start()
    for q in range(QC):
        for c in left_c[q][0] + [own_left[q][0]]:
            c.start()
    for c in bias_c[1] + [own_bias[1]]:
        c.start()
    for q in range(QC):
        for c in left_c[q][1] + [own_left[q][1]]:
            c.start()
    for c in wo_c + [wo_own]:
        c.start()

    wq_pad[...] = jnp.zeros_like(wq_pad)
    wkv_pad[...] = jnp.zeros_like(wkv_pad)
    wq_pad[:48, :] = q_w[...]
    wkv_pad[:48, :] = k_w[...]
    wkv_pad[VOFF : VOFF + 48, :] = v_w[...]
    wo_pad[VOFF : VOFF + 48, :] = o_w[...]

    @pl.loop(0, BR)
    def _(r):
        part = pl.ds(pl.multiple_of(r * BLK, BLK), BLK)
        normed = layer_norm(nodes[part, :].astype(F32))[0].astype(BF16)
        queries[r] = dot_nt(normed, wq_pad[...]).astype(BF16)
        kv_own[r] = dot_nt(normed, wkv_pad[...]).astype(BF16)
        cots[r] = dot_nt(cotan[part, :], wo_pad[...]).astype(BF16)

    @pl.loop(1, GRP)
    def _(to):
        write_stages(cols, grp, to, stage, kvstage)

    for n in range(14):
        kv_s[n] = kv_own[kvstage[n]]
    gpeers = [grp_peer(grp, offset) for offset in GRP_ORDER]
    kv_c = [
        to_grp(kv_s.at[pl.ds((o - 1) * 2, 2)], kv_r.at[pl.ds((o - 1) * 2, 2)], kv_ss.at[n], kv_rs.at[n], gpeers[n])
        for n, o in enumerate(GRP_ORDER)
    ]
    for c in kv_c:
        c.start()

    x_c = []
    for q in range(QC):
        for h in range(2):
            for c in right_c[q][h] + [own_right[q][h]]:
                c.wait()

        @pl.loop(0, 56)
        def _(n):
            xs[q][n] = right[q][stage[n]]

        x_c.append([
            to_grp(xs[q].at[pl.ds((o - 1) * 8, 8)], xr[q].at[pl.ds((o - 1) * 8, 8)], x_ss.at[q, n], x_rs.at[q, n], gpeers[n])
            for n, o in enumerate(GRP_ORDER)
        ])
        for c in x_c[q]:
            c.start()

    @pl.loop(0, NB)
    def _(b):
        write_places(cols, grp, b, place, kvplace)

    for c in kv_c:
        c.wait()
    for h in range(2):
        for c in bias_c[h] + [own_bias[h]]:
            c.wait()
    kv_all[:BR] = kv_own[...]
    kv_all[BR:] = kv_r[...]
    chain_bias = same[row]

    @pl.loop(0, BR)
    def _(r):
        here = chain[grp * BR + r]
        query = queries[r]
        cot = cots[r]
        top = jnp.full((BLK, 1), -jnp.inf, F32)
        for s in range(KS):
            kv = kv_all[kvplace[r * KS + s]]
            j = cols[s, grp * BR + r]
            extra = jnp.where(chain[j] == here, chain_bias, 0.0)
            part = dot_nt(query, kv) * (48 ** -0.5) + (bias[r * KS + s].astype(F32) + extra)
            part = jnp.where(mask[s, grp * BR + r] > 0, part, -jnp.inf)
            scores[s] = part
            gprobs[s] = dot_nt(cot, kv)
            top = jnp.maximum(top, jnp.max(part, axis=1, keepdims=True))
        total = jnp.zeros((BLK, 1), F32)
        for s in range(KS):
            part = jnp.exp(scores[s] - top)
            scores[s] = part
            total = total + jnp.sum(part, axis=1, keepdims=True)
        inverse = 1.0 / total
        dots = jnp.zeros((BLK, 1), F32)
        mix = jnp.zeros((BLK, PAD), F32)
        for s in range(KS):
            probs = scores[s] * inverse
            scores[s] = probs
            dots = dots + jnp.sum(probs * gprobs[s], axis=1, keepdims=True)
            mix = mix + dot_nn(probs.astype(BF16), kv_all[kvplace[r * KS + s]])
        for s in range(KS):
            grads[r * KS + s] = (scores[s] * (gprobs[s] - dots)).astype(BF16)
        mixed[pl.ds(pl.multiple_of(r * BLK, BLK), BLK), :] = mix.astype(BF16)

    slot = lambda p: pl.ds(pl.multiple_of(p * 8, 8), 8)
    rows32 = lambda p: pl.ds(pl.multiple_of(p * 32, 32), 32)
    mix_c = [
        to_row(mixed.at[rows32(p)], mixed_r.at[row], mix_ss.at[n], mix_rs.at[n], p) for n, p in enumerate(peers)
    ]
    mix_own = pltpu.make_async_copy(mixed.at[rows32(row)], mixed_r.at[row], own_s.at[0, 2 * QC + 2])
    grad_c = [
        to_row(grads.at[:, slot(p), :], grad_out.at[row], grad_ss.at[n], grad_rs.at[n], p)
        for n, p in enumerate(peers)
    ]
    grad_own = pltpu.make_async_copy(grads.at[:, mine, :], grad_out.at[row], own_s.at[0, 2 * QC + 3])
    for c in mix_c + [mix_own] + grad_c + [grad_own]:
        c.start()

    tri_c, tri_own = [], []
    for q in range(QC):
        for h in range(2):
            for c in left_c[q][h] + [own_left[q][h]]:
                c.wait()
        for c in x_c[q]:
            c.wait()

        @pl.loop(0, NB)
        def _(b):
            r = b // KS
            lhs, rhs = [], []
            for t in range(KS):
                code = place[b * KS + t]
                near = right[q][jnp.minimum(code, NB - 1)]
                far = xr[q][jnp.clip(code - NB, 0, 55)]
                block = jnp.where(code < NB, near, far)
                rhs.append(jnp.where(code < NB + 56, block, jnp.zeros_like(block)))
                lhs.append(left[q][r * KS + t])
            tri[q][b] = dot_nt(jnp.concatenate(lhs, axis=1), jnp.concatenate(rhs, axis=1)).astype(BF16)

        tri_c.append([
            to_row(tri[q].at[:, slot(p), :], tri_out.at[q, row], tri_ss.at[q, n], tri_rs.at[q, n], p)
            for n, p in enumerate(peers)
        ])
        tri_own.append(pltpu.make_async_copy(tri[q].at[:, mine, :], tri_out.at[q, row], own_s.at[1, 2 * QC + 1 + q]))
        for c in tri_c[q] + [tri_own[q]]:
            c.start()

    for c in wo_c + [wo_own] + mix_c + [mix_own]:
        c.wait()
    acc = nodes[rows32(row), :].astype(F32)
    for p in range(ROW):
        acc = acc + dot_nn(mixed_r[p], wo_all[p])
    node_out[...] = acc.astype(BF16)

    for c in grad_c + [grad_own]:
        c.wait()
    for q in range(QC):
        for c in tri_c[q] + [tri_own[q]]:
            c.wait()


def exchange(scalars, tensors, nodes):
    smem = pl.BlockSpec(memory_space=pltpu.SMEM)
    vmem = pl.BlockSpec(memory_space=pltpu.VMEM)
    anyspace = pl.BlockSpec(memory_space=pl.ANY)
    dma = pltpu.SemaphoreType.DMA
    blocks = lambda n: pltpu.VMEM((n, BLK, BLK), BF16)
    blocks_2d = pltpu.VMEM((BLK, BLK), BF16)
    n = ROW - 1
    scratch = (
        [blocks(NB)] * QC + [blocks(NB)] * QC + [blocks(NB)] * QC + [blocks(56)] * QC + [blocks(56)] * QC
        + [pltpu.VMEM((c, k, 8, BLK), BF16) for _, k in HALVES for c in (CH, CH, ROW)]
        + [pltpu.VMEM((k, 8, BLK, CZ), BF16) for _, k in HALVES]
        + [
            pltpu.VMEM((4 * CH + ROW, CZ), BF16), blocks_2d, pltpu.VMEM(((2 * CH + ROW) * 8, BLK), F32),
            pltpu.VMEM((8 * BLK, CZ), F32), pltpu.VMEM((8 * BLK, CZ), F32), pltpu.VMEM((8 * BLK, CZ), BF16),
            pltpu.SMEM((NB * KS,), jnp.int32), pltpu.SMEM((NB,), jnp.int32),
            pltpu.SMEM((56,), jnp.int32), pltpu.SMEM((14,), jnp.int32),
        ]
        + [
            blocks(NB), blocks(NB), blocks(BR), blocks(14), blocks(14), blocks(BR + 14), blocks(BR), blocks(BR),
            pltpu.VMEM((BR * BLK, PAD), BF16), pltpu.VMEM((ROW, 32, PAD), BF16),
            pltpu.VMEM((ROW, PAD, 768), BF16), pltpu.VMEM((PAD, 768), BF16), pltpu.VMEM((PAD, 768), BF16),
            pltpu.VMEM((PAD, 768), BF16), pltpu.VMEM((KS, BLK, BLK), F32), pltpu.VMEM((KS, BLK, BLK), F32),
        ]
        + [dma((2 * QC, n))] * 4 + [dma((QC, n))] * 2 + [dma((QC, 7))] * 2 + [dma((7,))] * 2 + [dma((n,))] * 6 + [dma((2, n))] * 2
        + [dma((2, 2 * QC + 1 + QC)), dma((2,))]
    )
    return pl.pallas_call(
        exchange_kernel,
        in_specs=[smem] * 4 + [anyspace] + [vmem] * 8,
        out_specs=[anyspace, anyspace, vmem],
        out_shape=[
            jax.ShapeDtypeStruct((QC, ROW, NB, 8, BLK), BF16),
            jax.ShapeDtypeStruct((ROW, NB, 8, BLK), BF16),
            jax.ShapeDtypeStruct((32, 768), BF16),
        ],
        scratch_shapes=scratch,
        compiler_params=pltpu.CompilerParams(
            collective_id=0, has_side_effects=True, vmem_limit_bytes=63 << 20
        ),
        name="exchange",
    )(*scalars, *tensors, *nodes)


def finish_kernel(
    pair, tri, grads, gate_w, out_w, bias_w, pair_out, pair_grad,
    weights, gates, ones, turned, shifted, inverse, hidden, gate, both,
):
    @pl.when(pl.program_id(0) == 0)
    def _():
        bias = bias_w[...].astype(F32)
        weights[...] = jnp.zeros_like(weights)
        weights[:CH, :CZ] = out_w[...] * 0.5
        weights[CH : CH + ROW, CZ:] = (bias - jnp.mean(bias, axis=1, keepdims=True)).astype(BF16)
        gates[...] = gate_w[...] * 0.5
        ones[...] = jnp.full_like(ones, 1.0 / CZ)
        turned[...] = jnp.zeros_like(turned)

    feats = pair[0].reshape(8 * BLK, CZ)
    shift_and_scale(feats, ones[...], shifted, inverse)
    shifted[...] = shifted[...] * inverse[...]
    gate[...] = dot_nn(shifted[...].astype(BF16), gates[...])

    sums = tri[:, 0].astype(F32)
    centred = sums - jnp.mean(sums, axis=0, keepdims=True)
    spread = jnp.mean(centred * centred, axis=0, keepdims=True)
    turned[: 8 * CH] = (centred * lax.rsqrt(spread + EPS)).reshape(8 * CH, BLK)
    turned[8 * CH : 8 * (CH + ROW)] = grads[:, 0].astype(F32).reshape(8 * ROW, BLK)
    for i in range(8):
        hidden[i * BLK : (i + 1) * BLK, :] = turned[pl.ds(i, PAD, stride=8), :].astype(BF16).T
    both[...] = dot_nn(hidden[...], weights[...])

    pair_out[0] = (
        (feats.astype(F32) + (jnp.tanh(gate[...]) + 1.0) * both[:, :CZ]).astype(BF16).reshape(8, BLK, CZ)
    )
    gate[...] = dot_nn((both[:, CZ:] * shifted[...]).astype(BF16), ones[...])
    pair_grad[0] = (
        (inverse[...] * (both[:, CZ:] - shifted[...] * gate[...])).astype(BF16).reshape(8, BLK, CZ)
    )


def finish(pair, tri, grads, gate_w, out_w, bias_w):
    by_block = lambda n: pl.BlockSpec((n, 1, 8, BLK), lambda b: (0, b, 0, 0))
    whole = lambda a: pl.BlockSpec(a.shape, lambda b: (0,) * a.ndim)
    pair_spec = pl.BlockSpec((1, 8, BLK, CZ), lambda b: (b, 0, 0, 0))
    return pl.pallas_call(
        finish_kernel,
        grid=(NB,),
        in_specs=[pair_spec, by_block(CH), by_block(ROW), whole(gate_w), whole(out_w), whole(bias_w)],
        out_specs=[pair_spec, pair_spec],
        out_shape=[jax.ShapeDtypeStruct(pair.shape, BF16)] * 2,
        scratch_shapes=[
            pltpu.VMEM((PAD, 2 * CZ), BF16),
            pltpu.VMEM((CZ, CZ), BF16),
            pltpu.VMEM((CZ, CZ), BF16),
            pltpu.VMEM((PAD * 8, BLK), F32),
            pltpu.VMEM((8 * BLK, CZ), F32),
            pltpu.VMEM((8 * BLK, CZ), F32),
            pltpu.VMEM((8 * BLK, PAD), BF16),
            pltpu.VMEM((8 * BLK, CZ), F32),
            pltpu.VMEM((8 * BLK, 2 * CZ), F32),
        ],
        compiler_params=pltpu.CompilerParams(vmem_limit_bytes=62 << 20),
        name="finish",
    )(pair, tri, grads, gate_w, out_w, bias_w)


def per_device(
    pair_feats,
    block_cols,
    attn_mask,
    chain_of_row,
    same_chain,
    node_feats,
    node_cotangent,
    tri_weight,
    gate_weight,
    tri_out_weight,
    bias_weight,
    query_weight,
    key_weight,
    value_weight,
    out_weight,
):
    pair = pair_feats.reshape(NB, 8, BLK, CZ)
    bias_t = bias_weight.T
    tri, grads, node_out = exchange(
        (block_cols.T, attn_mask.T, chain_of_row, same_chain),
        (pair, tri_weight, bias_t),
        (node_feats, node_cotangent, query_weight.T, key_weight.T, value_weight.T, out_weight),
    )
    pair_out, pair_grad = finish(
        pair, tri.reshape(CH, NB, 8, BLK), grads, gate_weight, tri_out_weight, bias_t
    )
    return pair_out.reshape(pair_feats.shape), node_out, pair_grad.reshape(pair_feats.shape)


def solution(mesh):
    pair_spec = P("grp", None, "row", None, None)
    node_spec = P("grp", None)
    in_specs = (
        (pair_spec,) + (P(),) * 4 + (node_spec,) * 2 + (P(),) * 4 + (P(None, "row"),) * 3 + (P("row", None),)
    )
    out_specs = (pair_spec, P(("grp", "row"), None), pair_spec)
    return jax.shard_map(per_device, mesh=mesh, in_specs=in_specs, out_specs=out_specs, check_vma=False)
```

```python
import jax
import jax.numpy as jnp
from jax import lax
from jax.experimental import pallas as pl
from jax.experimental.pallas import tpu as pltpu
from jax.sharding import PartitionSpec as P

F32 = jnp.float32
BF16 = jnp.bfloat16
MESH = pl.DeviceIdType.MESH
EPS = 1e-5
GRP, ROW = 8, 16
BR, KS, BLK, CZ, CH = 4, 6, 128, 128, 64
NB = BR * KS
QC = CH // ROW
PAD = 128
STEP = 2
VOFF = 64
PARTS = ((0, 6), (6, 10), (16, 8))
ROW_ORDER = (1, 3, 4, 12, 2, 8, 5, 15, 7, 13, 6, 14, 9, 11, 10)
GRP_ORDER = (2, 6, 4, 3, 7, 5, 1)


def row_peer(row, offset):
    z, y = row // 4, row % 4
    return ((z + offset // 4) % 4) * 4 + (y + offset % 4) % 4


def grp_peer(grp, offset):
    x, core = grp // 2, grp % 2
    return ((x + offset // 2) % 4) * 2 + (core + offset % 2) % 2


def layer_norm(values):
    center = jnp.mean(values, axis=-1, keepdims=True)
    shifted = values - center
    spread = jnp.mean(shifted * shifted, axis=-1, keepdims=True)
    inverse = lax.rsqrt(spread + EPS)
    return shifted * inverse, inverse


def dot_nt(a, b):
    return lax.dot_general(a, b, (((1,), (1,)), ((), ())), preferred_element_type=F32)


def dot_nn(a, b):
    return lax.dot_general(a, b, (((1,), (0,)), ((), ())), preferred_element_type=F32)


def dot_tn(a, b):
    return lax.dot_general(a, b, (((0,), (0,)), ((), ())), preferred_element_type=F32)


def i32(flag):
    return jnp.where(flag, 1, 0).astype(jnp.int32)


def named_ranks(cols, reader, owner):
    flags = [jnp.int32(0)] * BR
    for r in range(BR):
        for s in range(KS):
            c = cols[s, reader * BR + r]
            for l in range(BR):
                flags[l] = flags[l] | i32(c == owner * BR + l)
    ranks, count = [], jnp.int32(0)
    firsts = [jnp.int32(0), jnp.int32(0)]
    for l in range(BR):
        ranks.append(count)
        for a in range(2):
            firsts[a] = firsts[a] + l * flags[l] * i32(count == a)
        count = count + flags[l]
    return ranks, firsts


def pick(entries, index):
    out = jnp.int32(0)
    for n, entry in enumerate(entries):
        out = out + entry * i32(index == n)
    return out


def write_places(cols, grp, step, place, kvplace):
    inner = step // KS
    slot = step % KS
    j = cols[slot, grp * BR + inner]
    owner = j >> 2
    own = owner == grp
    ranks, _ = named_ranks(cols, grp, owner)
    offset = ((grp // 2 - owner // 2 + 4) % 4) * 2 + (grp % 2 - owner % 2 + 2) % 2
    rank_j = pick(ranks, j & 3)
    theirs = [cols[u, j] for u in range(KS)]
    for t in range(KS):
        c = cols[t, grp * BR + inner]
        found, far, count = jnp.int32(-1), jnp.int32(0), jnp.int32(0)
        for u in range(KS):
            hit = theirs[u] == c
            found = jnp.where(hit, u, found)
            far = jnp.where(hit, count, far)
            count = count + i32((theirs[u] >> 2) != owner)
        n = jnp.where((c >> 2) == owner, pick(ranks, c & 3), 2 + far)
        remote = NB + (offset - 1) * 8 + rank_j * 4 + n
        place[step * KS + t] = jnp.where(
            found >= 0, jnp.where(own, (j & 3) * KS + found, remote), NB + 56
        )
    kvplace[step] = jnp.where(own, j & 3, BR + (offset - 1) * 2 + rank_j)


def write_stages(cols, grp, to, stage, kvstage):
    reader = grp_peer(grp, to)
    _, firsts = named_ranks(cols, reader, grp)
    for a in range(2):
        near, far = [jnp.int32(0)] * 2, [jnp.int32(0)] * 2
        count = jnp.int32(0)
        for u in range(KS):
            c = cols[u, grp * BR + firsts[a]]
            away = i32((c >> 2) != grp)
            for n in range(2):
                near[n] = near[n] + u * i32(c == grp * BR + firsts[n])
                far[n] = far[n] + u * away * i32(count == n)
            count = count + away
        for n in range(2):
            stage[(to - 1) * 8 + a * 4 + n] = firsts[a] * KS + near[n]
            stage[(to - 1) * 8 + a * 4 + 2 + n] = firsts[a] * KS + far[n]
        kvstage[(to - 1) * 2 + a] = firsts[a]


def exchange_kernel(*refs):
    (
        cols, mask, chain, same, pair, tri_w, gate_w, bias_w, nodes, cotan, q_w, k_w, v_w, o_w,
        tri_out, grad_out, node_out, normed_out, gate_out, scale_out,
    ) = refs[:20]
    scr = list(refs[20:])
    take = lambda n: [scr.pop(0) for _ in range(n)]
    right = take(QC)
    left = take(QC)
    tri = take(QC)
    xs = take(QC)
    xr = take(QC)
    first_s = take(len(PARTS))
    rest_s = take(len(PARTS))
    left_s, bias_s = take(2)
    pair_v = take(len(PARTS))
    normed_v = take(len(PARTS))
    weights, ones, turned, shifted, inverse, gates, first_w, rest_w, place, kvplace, stage, kvstage = take(12)
    (bias, grads, kv_own, kv_s, kv_r, kv_all, queries, cots, mixed, mixed_r, wo_all,
     wq_pad, wkv_pad, wo_pad, scores, gprobs) = take(16)
    (right_ss, right_rs, left_ss, left_rs, tri_ss, tri_rs, x_ss, x_rs,
     kv_ss, kv_rs, grad_ss, grad_rs, mix_ss, mix_rs, wo_ss, wo_rs, bias_ss, bias_rs, own_s, pair_s, wx_ss, wx_rs, save_s) = take(23)

    grp = lax.axis_index("grp")
    row = lax.axis_index("row")
    mine = pl.ds(pl.multiple_of(row * 8, 8), 8)

    def to_row(src, dst, ss, rs, peer):
        return pltpu.make_async_remote_copy(
            src, dst, ss, rs, device_id=(grp, peer), device_id_type=MESH
        )

    def to_grp(src, dst, ss, rs, peer):
        return pltpu.make_async_remote_copy(
            src, dst, ss, rs, device_id=(peer, row), device_id_type=MESH
        )

    loads = [
        pltpu.make_async_copy(pair.at[pl.ds(first, count)], pair_v[h], pair_s.at[h])
        for h, (first, count) in enumerate(PARTS)
    ]
    for c in loads:
        c.start()

    barrier = pltpu.get_barrier_semaphore()
    for offset in ROW_ORDER:
        pl.semaphore_signal(barrier, inc=1, device_id=(grp, row_peer(row, offset)), device_id_type=MESH)
    for offset in GRP_ORDER:
        pl.semaphore_signal(barrier, inc=1, device_id=(grp_peer(grp, offset), row), device_id_type=MESH)
    wo_all[...] = jnp.zeros_like(wo_all)
    wo_pad[...] = jnp.zeros_like(wo_pad)
    weights[: 4 * CH, :] = (tri_w[...].astype(F32).T * 0.5).astype(BF16)
    weights[4 * CH :, :] = bias_w[...]
    ones[...] = jnp.full_like(ones, 1.0 / CZ)

    gates[...] = gate_w[...] * 0.5
    first_w[:ROW] = weights[2 * CH : 2 * CH + ROW]
    first_w[ROW:] = weights[3 * CH : 3 * CH + ROW]
    rest_w[: CH - ROW] = weights[2 * CH + ROW : 3 * CH]
    rest_w[CH - ROW :] = weights[3 * CH + ROW : 4 * CH]

    peers = [row_peer(row, offset) for offset in ROW_ORDER]

    def to_all(part, q, src, n_part):
        first, count = part
        here = pl.ds(first, count)
        return [
            to_row(src(p), right[q].at[here, mine, :], right_ss.at[n_part, n], right_rs.at[n_part, n], p)
            for n, p in enumerate(peers)
        ] + [pltpu.make_async_copy(src(row), right[q].at[here, mine, :], own_s.at[2, n_part])]

    right_c = [[to_all(part, 0, lambda p: first_s[h].at[p], h) for h, part in enumerate(PARTS)]] + [
        [
            to_all(part, q, lambda p: rest_s[h].at[(q - 1) * ROW + p], q * len(PARTS) + h)
            for h, part in enumerate(PARTS)
        ]
        for q in range(1, QC)
    ]
    left_c = [
        [
            to_row(left_s.at[q * ROW + p], left[q].at[:, mine, :], left_ss.at[q, n], left_rs.at[q, n], p)
            for n, p in enumerate(peers)
        ]
        + [pltpu.make_async_copy(left_s.at[q * ROW + row], left[q].at[:, mine, :], own_s.at[1, QC + q])]
        for q in range(QC)
    ]
    bias_c = [
        to_row(bias_s.at[p], bias.at[:, mine, :], bias_ss.at[n], bias_rs.at[n], p) for n, p in enumerate(peers)
    ] + [pltpu.make_async_copy(bias_s.at[row], bias.at[:, mine, :], own_s.at[0, 2 * QC])]
    chip = grp // 2
    fetches = chip < 3
    sixth = pl.ds(pl.multiple_of(lax.rem(grp, 6) * BLK, BLK), BLK)
    head_rows = pl.ds(VOFF, 48)
    wo_c = [
        to_row(o_w.at[:, sixth], wo_all.at[row, head_rows, sixth], wo_ss.at[n], wo_rs.at[n], p)
        for n, p in enumerate(peers)
    ]
    wo_own = pltpu.make_async_copy(o_w.at[:, sixth], wo_all.at[row, head_rows, sixth], own_s.at[0, 2 * QC + 1])

    def start(copies):
        for c in copies:
            c.start()

    for h, (first, count) in enumerate(PARTS):
        loads[h].wait()

        @pl.loop(0, count)
        def _(b):
            values = pair_v[h][b].reshape(8 * BLK, CZ)
            inverse[...] = dot_nn(values, ones[...])
            shifted[...] = values.astype(F32) - inverse[...]
            inverse[...] = dot_nn((shifted[...] * shifted[...]).astype(BF16), ones[...])
            normed_v[h][b] = (shifted[...] * lax.rsqrt(inverse[...] + EPS)).astype(BF16)
            for i in range(8):
                normed = normed_v[h][b, i * BLK : (i + 1) * BLK, :]
                projected = dot_nt(first_w[...], normed)
                turned[pl.ds(i, ROW, stride=8), :] = (jnp.tanh(projected[ROW:]) + 1.0) * projected[:ROW]
            first_s[h][:, b] = turned[: 8 * ROW].reshape(ROW, 8, BLK).astype(BF16)

        if h == 0:
            pl.semaphore_wait(barrier, 22)
        start(right_c[0][h])

    def project_rest(h):
        first, count = PARTS[h]

        @pl.loop(0, count)
        def _(b):
            for i in range(8):
                normed = normed_v[h][b, i * BLK : (i + 1) * BLK, :]
                projected = dot_nt(rest_w[...], normed)
                turned[pl.ds(i, CH - ROW, stride=8), :] = (
                    jnp.tanh(projected[CH - ROW :]) + 1.0
                ) * projected[: CH - ROW]
            rest_s[h][:, b] = turned[: 8 * (CH - ROW)].reshape(CH - ROW, 8, BLK).astype(BF16)

        for q in range(1, QC):
            start(right_c[q][h])

    project_rest(0)

    @pl.loop(1, GRP)
    def _(to):
        write_stages(cols, grp, to, stage, kvstage)

    saves = [
        pltpu.make_async_copy(normed_v[h], normed_out.at[pl.ds(first, count)], save_s.at[0, h])
        for h, (first, count) in enumerate(PARTS)
    ]
    start(saves)

    gpeers = [grp_peer(grp, offset) for offset in GRP_ORDER]
    x_c = []

    def exchange_channel(q):
        for part in right_c[q]:
            for c in part:
                c.wait()

        @pl.loop(0, 56)
        def _(n):
            xs[q][n] = right[q][stage[n]]

        x_c.append([
            to_grp(
                xs[q].at[pl.ds((o - 1) * 8, 8)], xr[q].at[pl.ds((o - 1) * 8, 8)],
                x_ss.at[q, n], x_rs.at[q, n], gpeers[n],
            )
            for n, o in enumerate(GRP_ORDER)
        ])
        start(x_c[q])

    exchange_channel(0)
    for h in range(1, len(PARTS)):
        project_rest(h)

    wq_pad[...] = jnp.zeros_like(wq_pad)
    wkv_pad[...] = jnp.zeros_like(wkv_pad)
    wq_pad[:48, :] = q_w[...]
    wkv_pad[:48, :] = k_w[...]
    wkv_pad[VOFF : VOFF + 48, :] = v_w[...]
    wo_pad[VOFF : VOFF + 48, :] = o_w[...]

    @pl.loop(0, BR)
    def _(r):
        part = pl.ds(pl.multiple_of(r * BLK, BLK), BLK)
        normed = layer_norm(nodes[part, :].astype(F32))[0].astype(BF16)
        queries[r] = dot_nt(normed, wq_pad[...]).astype(BF16)
        kv_own[r] = dot_nt(normed, wkv_pad[...]).astype(BF16)
        cots[r] = dot_nt(cotan[part, :], wo_pad[...]).astype(BF16)

    for n in range(14):
        kv_s[n] = kv_own[kvstage[n]]
    kv_c = [
        to_grp(kv_s.at[pl.ds((o - 1) * 2, 2)], kv_r.at[pl.ds((o - 1) * 2, 2)], kv_ss.at[n], kv_rs.at[n], gpeers[n])
        for n, o in enumerate(GRP_ORDER)
    ]
    start(kv_c)

    for h, (first, count) in enumerate(PARTS):

        @pl.loop(0, count)
        def _(b):
            for i in range(8):
                normed = normed_v[h][b, i * BLK : (i + 1) * BLK, :]
                projected = dot_nt(weights[: 2 * CH, :], normed)
                turned[pl.ds(i, CH, stride=8), :] = (jnp.tanh(projected[CH:]) + 1.0) * projected[:CH]
                turned[pl.ds(8 * CH + i, ROW, stride=8), :] = dot_nt(weights[4 * CH :, :], normed)
            left_s[:, first + b] = turned[: 8 * CH].reshape(CH, 8, BLK).astype(BF16)
            bias_s[:, first + b] = turned[8 * CH :].reshape(ROW, 8, BLK).astype(BF16)

    start(bias_c)
    for q in range(QC):
        start(left_c[q])

    @pl.when(fetches)
    def _():
        start(wo_c + [wo_own])

    exchange_channel(1)

    for h, (first, count) in enumerate(PARTS):

        @pl.loop(0, count)
        def _(b):
            values = pair_v[h][b].reshape(8 * BLK, CZ)
            shifted[...] = values.astype(F32) - dot_nn(values, ones[...])
            squares = (shifted[...] * shifted[...]).astype(BF16)
            for i in range(8):
                spread = dot_nt(ones[:8], squares[i * BLK : (i + 1) * BLK])
                scale_out[first + b, i : i + 1, :] = lax.rsqrt(spread[:1] + EPS)
            inverse[...] = jnp.tanh(dot_nn(normed_v[h][b], gates[...])) + 1.0
            pair_v[h][b] = inverse[...].astype(BF16).reshape(8, BLK, CZ)

        saves.append(pltpu.make_async_copy(pair_v[h], gate_out.at[pl.ds(first, count)], save_s.at[1, h]))
        saves[-1].start()

    exchange_channel(2)
    exchange_channel(3)

    @pl.loop(0, NB)
    def _(b):
        write_places(cols, grp, b, place, kvplace)

    for c in kv_c:
        c.wait()
    for c in bias_c:
        c.wait()
    kv_all[:BR] = kv_own[...]
    kv_all[BR:] = kv_r[...]
    chain_bias = same[row]

    @pl.loop(0, BR)
    def _(r):
        here = chain[grp * BR + r]
        query = queries[r]
        cot = cots[r]
        top = jnp.full((BLK, 1), -jnp.inf, F32)
        for s in range(KS):
            kv = kv_all[kvplace[r * KS + s]]
            j = cols[s, grp * BR + r]
            extra = jnp.where(chain[j] == here, chain_bias, 0.0)
            part = dot_nt(query, kv) * (48 ** -0.5) + (bias[r * KS + s].astype(F32) + extra)
            part = jnp.where(mask[s, grp * BR + r] > 0, part, -jnp.inf)
            scores[s] = part
            gprobs[s] = dot_nt(cot, kv)
            top = jnp.maximum(top, jnp.max(part, axis=1, keepdims=True))
        total = jnp.zeros((BLK, 1), F32)
        for s in range(KS):
            part = jnp.exp(scores[s] - top)
            scores[s] = part
            total = total + jnp.sum(part, axis=1, keepdims=True)
        inverse = 1.0 / total
        dots = jnp.zeros((BLK, 1), F32)
        mix = jnp.zeros((BLK, PAD), F32)
        for s in range(KS):
            probs = scores[s] * inverse
            scores[s] = probs
            dots = dots + jnp.sum(probs * gprobs[s], axis=1, keepdims=True)
            mix = mix + dot_nn(probs.astype(BF16), kv_all[kvplace[r * KS + s]])
        for s in range(KS):
            grads[r * KS + s] = (scores[s] * (gprobs[s] - dots)).astype(BF16)
        mixed[pl.ds(pl.multiple_of(r * BLK, BLK), BLK), :] = mix.astype(BF16)

    slot = lambda p: pl.ds(pl.multiple_of(p * 8, 8), 8)
    rows32 = lambda p: pl.ds(pl.multiple_of(p * 32, 32), 32)
    mix_c = [
        to_row(mixed.at[rows32(p)], mixed_r.at[row], mix_ss.at[n], mix_rs.at[n], p) for n, p in enumerate(peers)
    ]
    mix_own = pltpu.make_async_copy(mixed.at[rows32(row)], mixed_r.at[row], own_s.at[0, 2 * QC + 2])
    grad_c = [
        to_row(grads.at[:, slot(p), :], grad_out.at[:, row], grad_ss.at[n], grad_rs.at[n], p)
        for n, p in enumerate(peers)
    ]
    grad_own = pltpu.make_async_copy(grads.at[:, mine, :], grad_out.at[:, row], own_s.at[0, 2 * QC + 3])
    for c in mix_c + [mix_own] + grad_c + [grad_own]:
        c.start()

    tri_c = []
    wx_c = [
        to_grp(wo_all.at[:, head_rows, sixth], wo_all.at[:, head_rows, sixth], wx_ss.at[n], wx_rs.at[n], gpeers[n])
        for n in range(7)
    ]
    for q in range(QC):
        if q == QC - 1:

            @pl.when(fetches)
            def _():
                for c in wo_c + [wo_own]:
                    c.wait()
                for c in wx_c:
                    c.start()

        for c in left_c[q]:
            c.wait()
        for c in x_c[q]:
            c.wait()

        cuts = ((0, NB),) if q < QC - 1 else ((0, NB // 2), (NB // 2, NB // 2))
        for h, (first, count) in enumerate(cuts):

            @pl.loop(first, first + count)
            def _(b):
                r = b // KS
                lhs, rhs = [], []
                for t in range(KS):
                    code = place[b * KS + t]
                    near = right[q][jnp.minimum(code, NB - 1)]
                    far = xr[q][jnp.clip(code - NB, 0, 55)]
                    block = jnp.where(code < NB, near, far)
                    rhs.append(jnp.where(code < NB + 56, block, jnp.zeros_like(block)))
                    lhs.append(left[q][r * KS + t])
                tri[q][b] = dot_nt(jnp.concatenate(lhs, axis=1), jnp.concatenate(rhs, axis=1)).astype(BF16)

            here = pl.ds(first, count)
            tri_c.append([
                to_row(tri[q].at[here, slot(p), :], tri_out.at[here, q, row], tri_ss.at[q + h, n], tri_rs.at[q + h, n], p)
                for n, p in enumerate(peers)
            ] + [pltpu.make_async_copy(tri[q].at[here, mine, :], tri_out.at[here, q, row], own_s.at[1, 8 + q + h])])
            start(tri_c[-1])

    for c in mix_c + [mix_own]:
        c.wait()

    @pl.when(fetches)
    def _():
        for c in wx_c:
            c.wait_send()

    for n, o in enumerate(GRP_ORDER):

        @pl.when((chip - o // 2 + 4) % 4 < 3)
        def _():
            wx_c[n].wait_recv()

    acc = nodes[rows32(row), :].astype(F32)
    for p in range(ROW):
        acc = acc + dot_nn(mixed_r[p], wo_all[p])
    node_out[...] = acc.astype(BF16)

    for c in saves + grad_c + [grad_own]:
        c.wait()
    for part in tri_c:
        for c in part:
            c.wait()


def exchange(scalars, tensors, nodes):
    smem = pl.BlockSpec(memory_space=pltpu.SMEM)
    vmem = pl.BlockSpec(memory_space=pltpu.VMEM)
    anyspace = pl.BlockSpec(memory_space=pl.ANY)
    dma = pltpu.SemaphoreType.DMA
    blocks = lambda n: pltpu.VMEM((n, BLK, BLK), BF16)
    blocks_2d = pltpu.VMEM((BLK, BLK), BF16)
    n = ROW - 1
    scratch = (
        [blocks(NB)] * QC + [blocks(NB)] * QC + [blocks(NB)] * QC + [blocks(56)] * QC + [blocks(56)] * QC
        + [pltpu.VMEM((ROW, k, 8, BLK), BF16) for _, k in PARTS]
        + [pltpu.VMEM((CH - ROW, k, 8, BLK), BF16) for _, k in PARTS]
        + [pltpu.VMEM((CH, NB, 8, BLK), BF16), pltpu.VMEM((ROW, NB, 8, BLK), BF16)]
        + [pltpu.VMEM((k, 8, BLK, CZ), BF16) for _, k in PARTS]
        + [pltpu.VMEM((k, 8 * BLK, CZ), BF16) for _, k in PARTS]
        + [
            pltpu.VMEM((4 * CH + ROW, CZ), BF16), blocks_2d, pltpu.VMEM(((CH + ROW) * 8, BLK), F32),
            pltpu.VMEM((8 * BLK, CZ), F32), pltpu.VMEM((8 * BLK, CZ), F32), blocks_2d,
            pltpu.VMEM((2 * ROW, CZ), BF16), pltpu.VMEM((2 * (CH - ROW), CZ), BF16),
            pltpu.SMEM((NB * KS,), jnp.int32), pltpu.SMEM((NB,), jnp.int32),
            pltpu.SMEM((56,), jnp.int32), pltpu.SMEM((14,), jnp.int32),
        ]
        + [
            blocks(NB), blocks(NB), blocks(BR), blocks(14), blocks(14), blocks(BR + 14), blocks(BR), blocks(BR),
            pltpu.VMEM((BR * BLK, PAD), BF16), pltpu.VMEM((ROW, 32, PAD), BF16),
            pltpu.VMEM((ROW, PAD, 768), BF16), pltpu.VMEM((PAD, 768), BF16), pltpu.VMEM((PAD, 768), BF16),
            pltpu.VMEM((PAD, 768), BF16), pltpu.VMEM((KS, BLK, BLK), F32), pltpu.VMEM((KS, BLK, BLK), F32),
        ]
        + [dma((len(PARTS) * QC, n))] * 2 + [dma((QC, n))] * 2 + [dma((QC + 1, n))] * 2 + [dma((QC, 7))] * 2 + [dma((7,))] * 2 + [dma((n,))] * 8
        + [dma((len(PARTS), 2 * QC + 1 + QC)), dma((len(PARTS),)), dma((7,)), dma((7,)), dma((2, len(PARTS)))]
    )
    return pl.pallas_call(
        exchange_kernel,
        in_specs=[smem] * 4 + [anyspace] + [vmem] * 9,
        out_specs=[anyspace, anyspace, vmem, anyspace, anyspace, vmem],
        out_shape=[
            jax.ShapeDtypeStruct((NB, QC, ROW, 8, BLK), BF16),
            jax.ShapeDtypeStruct((NB, ROW, 8, BLK), BF16),
            jax.ShapeDtypeStruct((32, 768), BF16),
            jax.ShapeDtypeStruct((NB, 8 * BLK, CZ), BF16),
            jax.ShapeDtypeStruct((NB, 8, BLK, CZ), BF16),
            jax.ShapeDtypeStruct((NB, 8, BLK), F32),
        ],
        scratch_shapes=scratch,
        compiler_params=pltpu.CompilerParams(
            collective_id=0, has_side_effects=True, vmem_limit_bytes=63 << 20
        ),
        name="exchange",
    )(*scalars, *tensors, *nodes)


def finish_kernel(
    pair, tri, grads, normed, gate, scale, out_w, bias_w, pair_out, pair_grad,
    weights, ones, turned, hidden, both, along,
):
    @pl.when(pl.program_id(0) == 0)
    def _():
        bias = bias_w[...].astype(F32)
        weights[...] = jnp.zeros_like(weights)
        weights[:CH, :CZ] = out_w[...] * 0.5
        weights[CH : CH + ROW, CZ:] = (bias - jnp.mean(bias, axis=1, keepdims=True)).astype(BF16)
        ones[...] = jnp.full_like(ones, 1.0 / CZ)
        turned[...] = jnp.zeros_like(turned)

    def norm(k):
        sums = tri[k].astype(F32)
        centred = sums - jnp.mean(sums, axis=0, keepdims=True)
        spread = jnp.mean(centred * centred, axis=0, keepdims=True)
        turned[k, : 8 * CH] = (centred * lax.rsqrt(spread + EPS)).reshape(8 * CH, BLK)
        turned[k, 8 * CH : 8 * (CH + ROW)] = (grads[k].astype(F32) * scale[k]).reshape(8 * ROW, BLK)

    def turn(k):
        for i in range(8):
            hidden[k, i * BLK : (i + 1) * BLK, :] = turned[k, pl.ds(i, PAD, stride=8), :].astype(BF16).T

    def product(k):
        both[k] = dot_nn(hidden[k], weights[...])

    def project(k):
        along[k] = dot_nn(both[k, :, CZ:].astype(BF16) * normed[k], ones[...])

    def store(k):
        for i in range(8):
            rows = slice(i * BLK, (i + 1) * BLK)
            pair_out[k, i] = (
                pair[k, i].astype(F32) + gate[k, i].astype(F32) * both[k, rows, :CZ]
            ).astype(BF16)
            pair_grad[k, i] = (
                both[k, rows, CZ:] - normed[k, rows, :].astype(F32) * along[k, rows, :]
            ).astype(BF16)

    norm(0)
    for k in range(STEP):
        turn(k)
        if k + 1 < STEP:
            norm(k + 1)
        product(k)
        if k > 0:
            store(k - 1)
        project(k)
    store(STEP - 1)


def finish(pair, tri, grads, normed, gate, scale, out_w, bias_w):
    by_block = lambda a: pl.BlockSpec((STEP,) + a.shape[1:], lambda b: (b,) + (0,) * (a.ndim - 1))
    whole = lambda a: pl.BlockSpec(a.shape, lambda b: (0,) * a.ndim)
    return pl.pallas_call(
        finish_kernel,
        grid=(NB // STEP,),
        in_specs=[by_block(a) for a in (pair, tri, grads, normed, gate, scale)] + [whole(out_w), whole(bias_w)],
        out_specs=[by_block(pair), by_block(pair)],
        out_shape=[jax.ShapeDtypeStruct(pair.shape, BF16)] * 2,
        scratch_shapes=[
            pltpu.VMEM((PAD, 2 * CZ), BF16),
            pltpu.VMEM((CZ, CZ), BF16),
            pltpu.VMEM((STEP, PAD * 8, BLK), F32),
            pltpu.VMEM((STEP, 8 * BLK, PAD), BF16),
            pltpu.VMEM((STEP, 8 * BLK, 2 * CZ), F32),
            pltpu.VMEM((STEP, 8 * BLK, CZ), F32),
        ],
        compiler_params=pltpu.CompilerParams(vmem_limit_bytes=62 << 20),
        name="finish",
    )(pair, tri, grads, normed, gate, scale, out_w, bias_w)


def per_device(
    pair_feats,
    block_cols,
    attn_mask,
    chain_of_row,
    same_chain,
    node_feats,
    node_cotangent,
    tri_weight,
    gate_weight,
    tri_out_weight,
    bias_weight,
    query_weight,
    key_weight,
    value_weight,
    out_weight,
):
    pair = pair_feats.reshape(NB, 8, BLK, CZ)
    bias_t = bias_weight.T
    tri, grads, node_out, normed, gate, scale = exchange(
        (block_cols.T, attn_mask.T, chain_of_row, same_chain),
        (pair, tri_weight, gate_weight, bias_t),
        (node_feats, node_cotangent, query_weight.T, key_weight.T, value_weight.T, out_weight),
    )
    pair_out, pair_grad = finish(
        pair, tri.reshape(NB, CH, 8, BLK), grads, normed, gate, scale, tri_out_weight, bias_t
    )
    return pair_out.reshape(pair_feats.shape), node_out, pair_grad.reshape(pair_feats.shape)


def solution(mesh):
    pair_spec = P("grp", None, "row", None, None)
    node_spec = P("grp", None)
    in_specs = (
        (pair_spec,) + (P(),) * 4 + (node_spec,) * 2 + (P(),) * 4 + (P(None, "row"),) * 3 + (P("row", None),)
    )
    out_specs = (pair_spec, P(("grp", "row"), None), pair_spec)
    return jax.shard_map(per_device, mesh=mesh, in_specs=in_specs, out_specs=out_specs, check_vma=False)
```

```python
import jax
import jax.numpy as jnp
from jax import lax
from jax.experimental import pallas as pl
from jax.experimental.pallas import tpu as pltpu
from jax.sharding import PartitionSpec as P

F32 = jnp.float32
BF16 = jnp.bfloat16
MESH = pl.DeviceIdType.MESH
EPS = 1e-5
GRP, ROW = 8, 16
BR, KS, BLK, CZ, CH = 4, 6, 128, 128, 64
NB = BR * KS
QC = CH // ROW
PAD = 128
STEP = 2
VOFF = 64
PARTS = ((0, 6), (6, 10), (16, 8))
ROW_ORDER = (1, 3, 4, 12, 2, 8, 5, 15, 7, 13, 6, 14, 9, 11, 10)
GRP_ORDER = (2, 6, 4, 3, 7, 5, 1)


def row_peer(row, offset):
    z, y = row // 4, row % 4
    return ((z + offset // 4) % 4) * 4 + (y + offset % 4) % 4


def grp_peer(grp, offset):
    x, core = grp // 2, grp % 2
    return ((x + offset // 2) % 4) * 2 + (core + offset % 2) % 2


def layer_norm(values):
    center = jnp.mean(values, axis=-1, keepdims=True)
    shifted = values - center
    spread = jnp.mean(shifted * shifted, axis=-1, keepdims=True)
    inverse = lax.rsqrt(spread + EPS)
    return shifted * inverse, inverse


def dot_nt(a, b):
    return lax.dot_general(a, b, (((1,), (1,)), ((), ())), preferred_element_type=F32)


def dot_nn(a, b):
    return lax.dot_general(a, b, (((1,), (0,)), ((), ())), preferred_element_type=F32)


def dot_tn(a, b):
    return lax.dot_general(a, b, (((0,), (0,)), ((), ())), preferred_element_type=F32)


def i32(flag):
    return jnp.where(flag, 1, 0).astype(jnp.int32)


def named_ranks(cols, reader, owner):
    flags = [jnp.int32(0)] * BR
    for r in range(BR):
        for s in range(KS):
            c = cols[s, reader * BR + r]
            for l in range(BR):
                flags[l] = flags[l] | i32(c == owner * BR + l)
    ranks, count = [], jnp.int32(0)
    firsts = [jnp.int32(0), jnp.int32(0)]
    for l in range(BR):
        ranks.append(count)
        for a in range(2):
            firsts[a] = firsts[a] + l * flags[l] * i32(count == a)
        count = count + flags[l]
    return ranks, firsts


def pick(entries, index):
    out = jnp.int32(0)
    for n, entry in enumerate(entries):
        out = out + entry * i32(index == n)
    return out


def write_places(cols, grp, step, place, kvplace):
    inner = step // KS
    slot = step % KS
    j = cols[slot, grp * BR + inner]
    owner = j >> 2
    own = owner == grp
    ranks, _ = named_ranks(cols, grp, owner)
    offset = ((grp // 2 - owner // 2 + 4) % 4) * 2 + (grp % 2 - owner % 2 + 2) % 2
    rank_j = pick(ranks, j & 3)
    theirs = [cols[u, j] for u in range(KS)]
    for t in range(KS):
        c = cols[t, grp * BR + inner]
        found, far, count = jnp.int32(-1), jnp.int32(0), jnp.int32(0)
        for u in range(KS):
            hit = theirs[u] == c
            found = jnp.where(hit, u, found)
            far = jnp.where(hit, count, far)
            count = count + i32((theirs[u] >> 2) != owner)
        n = jnp.where((c >> 2) == owner, pick(ranks, c & 3), 2 + far)
        remote = NB + (offset - 1) * 8 + rank_j * 4 + n
        place[step * KS + t] = jnp.where(
            found >= 0, jnp.where(own, (j & 3) * KS + found, remote), NB + 56
        )
    kvplace[step] = jnp.where(own, j & 3, BR + (offset - 1) * 2 + rank_j)


def write_stages(cols, grp, to, stage, kvstage):
    reader = grp_peer(grp, to)
    _, firsts = named_ranks(cols, reader, grp)
    for a in range(2):
        near, far = [jnp.int32(0)] * 2, [jnp.int32(0)] * 2
        count = jnp.int32(0)
        for u in range(KS):
            c = cols[u, grp * BR + firsts[a]]
            away = i32((c >> 2) != grp)
            for n in range(2):
                near[n] = near[n] + u * i32(c == grp * BR + firsts[n])
                far[n] = far[n] + u * away * i32(count == n)
            count = count + away
        for n in range(2):
            stage[(to - 1) * 8 + a * 4 + n] = firsts[a] * KS + near[n]
            stage[(to - 1) * 8 + a * 4 + 2 + n] = firsts[a] * KS + far[n]
        kvstage[(to - 1) * 2 + a] = firsts[a]


def exchange_kernel(*refs):
    (
        cols, mask, chain, same, pair, tri_w, gate_w, bias_w, nodes, cotan, q_w, k_w, v_w, o_w,
        tri_out, grad_out, node_out, normed_out, gate_out, scale_out,
    ) = refs[:20]
    scr = list(refs[20:])
    take = lambda n: [scr.pop(0) for _ in range(n)]
    right = take(QC)
    left = take(QC)
    tri = take(QC)
    xs = take(QC)
    xr = take(QC)
    first_s = take(len(PARTS))
    rest_s = take(len(PARTS))
    left_s, bias_s = take(2)
    pair_v = take(len(PARTS))
    normed_v = take(len(PARTS))
    weights, ones, turned, shifted, inverse, gates, first_w, rest_w, place, kvplace, stage, kvstage = take(12)
    (bias, grads, kv_own, kv_s, kv_r, kv_all, queries, cots, mixed, mixed_r, wo_all,
     wq_pad, wkv_pad, wo_pad, scores, gprobs) = take(16)
    (right_ss, right_rs, left_ss, left_rs, tri_ss, tri_rs, x_ss, x_rs,
     kv_ss, kv_rs, grad_ss, grad_rs, mix_ss, mix_rs, wo_ss, wo_rs, bias_ss, bias_rs, own_s, pair_s, wx_ss, wx_rs, save_s) = take(23)

    grp = lax.axis_index("grp")
    row = lax.axis_index("row")
    mine = pl.ds(pl.multiple_of(row * 8, 8), 8)

    def to_row(src, dst, ss, rs, peer):
        return pltpu.make_async_remote_copy(
            src, dst, ss, rs, device_id=(grp, peer), device_id_type=MESH
        )

    def to_grp(src, dst, ss, rs, peer):
        return pltpu.make_async_remote_copy(
            src, dst, ss, rs, device_id=(peer, row), device_id_type=MESH
        )

    loads = [
        pltpu.make_async_copy(pair.at[pl.ds(first, count)], pair_v[h], pair_s.at[h])
        for h, (first, count) in enumerate(PARTS)
    ]
    for c in loads:
        c.start()

    barrier = pltpu.get_barrier_semaphore()
    for offset in ROW_ORDER:
        pl.semaphore_signal(barrier, inc=1, device_id=(grp, row_peer(row, offset)), device_id_type=MESH)
    for offset in GRP_ORDER:
        pl.semaphore_signal(barrier, inc=1, device_id=(grp_peer(grp, offset), row), device_id_type=MESH)
    weights[: 4 * CH, :] = (tri_w[...].astype(F32).T * 0.5).astype(BF16)
    weights[4 * CH :, :] = bias_w[...]
    ones[...] = jnp.full_like(ones, 1.0 / CZ)

    gates[...] = gate_w[...] * 0.5
    first_w[:ROW] = weights[2 * CH : 2 * CH + ROW]
    first_w[ROW:] = weights[3 * CH : 3 * CH + ROW]
    rest_w[: CH - ROW] = weights[2 * CH + ROW : 3 * CH]
    rest_w[CH - ROW :] = weights[3 * CH + ROW : 4 * CH]

    peers = [row_peer(row, offset) for offset in ROW_ORDER]

    def to_all(part, q, src, n_part):
        first, count = part
        here = pl.ds(first, count)
        return [
            to_row(src(p), right[q].at[here, mine, :], right_ss.at[n_part, n], right_rs.at[n_part, n], p)
            for n, p in enumerate(peers)
        ] + [pltpu.make_async_copy(src(row), right[q].at[here, mine, :], own_s.at[2, n_part])]

    right_c = [[to_all(part, 0, lambda p: first_s[h].at[p], h) for h, part in enumerate(PARTS)]] + [
        [
            to_all(part, q, lambda p: rest_s[h].at[(q - 1) * ROW + p], q * len(PARTS) + h)
            for h, part in enumerate(PARTS)
        ]
        for q in range(1, QC)
    ]
    left_c = [
        [
            to_row(left_s.at[q * ROW + p], left[q].at[:, mine, :], left_ss.at[q, n], left_rs.at[q, n], p)
            for n, p in enumerate(peers)
        ]
        + [pltpu.make_async_copy(left_s.at[q * ROW + row], left[q].at[:, mine, :], own_s.at[1, QC + q])]
        for q in range(QC)
    ]
    bias_c = [
        to_row(bias_s.at[p], bias.at[:, mine, :], bias_ss.at[n], bias_rs.at[n], p) for n, p in enumerate(peers)
    ] + [pltpu.make_async_copy(bias_s.at[row], bias.at[:, mine, :], own_s.at[0, 2 * QC])]
    chip = grp // 2
    fetches = chip < 3
    sixth = pl.ds(pl.multiple_of(lax.rem(grp, 6) * BLK, BLK), BLK)
    wo_c = [
        to_row(o_w.at[:, sixth], wo_all.at[row, :, sixth], wo_ss.at[n], wo_rs.at[n], p)
        for n, p in enumerate(peers)
    ]
    wo_own = pltpu.make_async_copy(o_w.at[:, sixth], wo_all.at[row, :, sixth], own_s.at[0, 2 * QC + 1])

    def start(copies):
        for c in copies:
            c.start()

    def project_rest(h):
        first, count = PARTS[h]

        @pl.loop(0, count)
        def _(b):
            for i in range(8):
                normed = normed_v[h][b, i * BLK : (i + 1) * BLK, :]
                projected = dot_nt(rest_w[...], normed)
                turned[pl.ds(i, CH - ROW, stride=8), :] = (
                    jnp.tanh(projected[CH - ROW :]) + 1.0
                ) * projected[: CH - ROW]
            rest_s[h][:, b] = turned[: 8 * (CH - ROW)].reshape(CH - ROW, 8, BLK).astype(BF16)

        for q in range(1, QC):
            start(right_c[q][h])

    gpeers = [grp_peer(grp, offset) for offset in GRP_ORDER]
    kv_c = []

    def node_part():
        @pl.loop(1, GRP)
        def _(to):
            write_stages(cols, grp, to, stage, kvstage)

        wo_pad[...] = jnp.zeros_like(wo_pad)
        wq_pad[...] = jnp.zeros_like(wq_pad)
        wkv_pad[...] = jnp.zeros_like(wkv_pad)
        wq_pad[:48, :] = q_w[...]
        wkv_pad[:48, :] = k_w[...]
        wkv_pad[VOFF : VOFF + 48, :] = v_w[...]
        wo_pad[VOFF : VOFF + 48, :] = o_w[...]

        @pl.loop(0, BR)
        def _(r):
            part = pl.ds(pl.multiple_of(r * BLK, BLK), BLK)
            normed = layer_norm(nodes[part, :].astype(F32))[0].astype(BF16)
            queries[r] = dot_nt(normed, wq_pad[...]).astype(BF16)
            kv_own[r] = dot_nt(normed, wkv_pad[...]).astype(BF16)
            cots[r] = dot_nt(cotan[part, :], wo_pad[...]).astype(BF16)

        for n in range(14):
            kv_s[n] = kv_own[kvstage[n]]
        kv_c[:] = [
            to_grp(kv_s.at[pl.ds((o - 1) * 2, 2)], kv_r.at[pl.ds((o - 1) * 2, 2)], kv_ss.at[n], kv_rs.at[n], gpeers[n])
            for n, o in enumerate(GRP_ORDER)
        ]
        start(kv_c)

    for h, (first, count) in enumerate(PARTS):
        loads[h].wait()

        @pl.loop(0, count)
        def _(b):
            values = pair_v[h][b].reshape(8 * BLK, CZ)
            inverse[...] = dot_nn(values, ones[...])
            shifted[...] = values.astype(F32) - inverse[...]
            inverse[...] = dot_nn((shifted[...] * shifted[...]).astype(BF16), ones[...])
            normed_v[h][b] = (shifted[...] * lax.rsqrt(inverse[...] + EPS)).astype(BF16)
            for i in range(8):
                normed = normed_v[h][b, i * BLK : (i + 1) * BLK, :]
                projected = dot_nt(first_w[...], normed)
                turned[pl.ds(i, ROW, stride=8), :] = (jnp.tanh(projected[ROW:]) + 1.0) * projected[:ROW]
            first_s[h][:, b] = turned[: 8 * ROW].reshape(ROW, 8, BLK).astype(BF16)

        if h == 0:
            pl.semaphore_wait(barrier, 22)
        start(right_c[0][h])
        if h == 0:
            project_rest(0)
            node_part()


    saves = [
        pltpu.make_async_copy(normed_v[h], normed_out.at[pl.ds(first, count)], save_s.at[0, h])
        for h, (first, count) in enumerate(PARTS)
    ]
    start(saves)

    x_c = []

    def exchange_channel(q):
        for part in right_c[q]:
            for c in part:
                c.wait()

        @pl.loop(0, 56)
        def _(n):
            xs[q][n] = right[q][stage[n]]

        x_c.append([
            to_grp(
                xs[q].at[pl.ds((o - 1) * 8, 8)], xr[q].at[pl.ds((o - 1) * 8, 8)],
                x_ss.at[q, n], x_rs.at[q, n], gpeers[n],
            )
            for n, o in enumerate(GRP_ORDER)
        ])
        start(x_c[q])

    exchange_channel(0)
    for h in range(1, len(PARTS)):
        project_rest(h)

    for h, (first, count) in enumerate(PARTS):

        @pl.loop(0, count)
        def _(b):
            for i in range(8):
                normed = normed_v[h][b, i * BLK : (i + 1) * BLK, :]
                projected = dot_nt(weights[: 2 * CH, :], normed)
                turned[pl.ds(i, CH, stride=8), :] = (jnp.tanh(projected[CH:]) + 1.0) * projected[:CH]
                turned[pl.ds(8 * CH + i, ROW, stride=8), :] = dot_nt(weights[4 * CH :, :], normed)
            left_s[:, first + b] = turned[: 8 * CH].reshape(CH, 8, BLK).astype(BF16)
            bias_s[:, first + b] = turned[8 * CH :].reshape(ROW, 8, BLK).astype(BF16)

    start(bias_c)
    for q in range(QC):
        start(left_c[q])

    @pl.when(fetches)
    def _():
        start(wo_c + [wo_own])

    exchange_channel(1)

    for h, (first, count) in enumerate(PARTS):

        @pl.loop(0, count)
        def _(b):
            values = pair_v[h][b].reshape(8 * BLK, CZ)
            shifted[...] = values.astype(F32) - dot_nn(values, ones[...])
            squares = (shifted[...] * shifted[...]).astype(BF16)
            for i in range(8):
                spread = dot_nt(ones[:8], squares[i * BLK : (i + 1) * BLK])
                scale_out[first + b, i : i + 1, :] = lax.rsqrt(spread[:1] + EPS)
            inverse[...] = jnp.tanh(dot_nn(normed_v[h][b], gates[...])) + 1.0
            pair_v[h][b] = inverse[...].astype(BF16).reshape(8, BLK, CZ)

        saves.append(pltpu.make_async_copy(pair_v[h], gate_out.at[pl.ds(first, count)], save_s.at[1, h]))
        saves[-1].start()

    exchange_channel(2)
    exchange_channel(3)

    @pl.loop(0, NB)
    def _(b):
        write_places(cols, grp, b, place, kvplace)

    for c in kv_c:
        c.wait()
    for c in bias_c:
        c.wait()
    kv_all[:BR] = kv_own[...]
    kv_all[BR:] = kv_r[...]
    chain_bias = same[row]

    @pl.loop(0, BR)
    def _(r):
        here = chain[grp * BR + r]
        query = queries[r]
        cot = cots[r]
        top = jnp.full((BLK, 1), -jnp.inf, F32)
        for s in range(KS):
            kv = kv_all[kvplace[r * KS + s]]
            j = cols[s, grp * BR + r]
            extra = jnp.where(chain[j] == here, chain_bias, 0.0)
            part = dot_nt(query, kv) * (48 ** -0.5) + (bias[r * KS + s].astype(F32) + extra)
            part = jnp.where(mask[s, grp * BR + r] > 0, part, -jnp.inf)
            scores[s] = part
            gprobs[s] = dot_nt(cot, kv)
            top = jnp.maximum(top, jnp.max(part, axis=1, keepdims=True))
        total = jnp.zeros((BLK, 1), F32)
        for s in range(KS):
            part = jnp.exp(scores[s] - top)
            scores[s] = part
            total = total + jnp.sum(part, axis=1, keepdims=True)
        inverse = 1.0 / total
        dots = jnp.zeros((BLK, 1), F32)
        mix = jnp.zeros((BLK, PAD), F32)
        for s in range(KS):
            probs = scores[s] * inverse
            scores[s] = probs
            dots = dots + jnp.sum(probs * gprobs[s], axis=1, keepdims=True)
            mix = mix + dot_nn(probs.astype(BF16), kv_all[kvplace[r * KS + s]])
        for s in range(KS):
            grads[r * KS + s] = (scores[s] * (gprobs[s] - dots)).astype(BF16)
        mixed[pl.ds(pl.multiple_of(r * BLK, BLK), BLK), :] = mix.astype(BF16)

    slot = lambda p: pl.ds(pl.multiple_of(p * 8, 8), 8)
    rows32 = lambda p: pl.ds(pl.multiple_of(p * 32, 32), 32)
    mix_c = [
        to_row(mixed.at[rows32(p)], mixed_r.at[row], mix_ss.at[n], mix_rs.at[n], p) for n, p in enumerate(peers)
    ]
    mix_own = pltpu.make_async_copy(mixed.at[rows32(row)], mixed_r.at[row], own_s.at[0, 2 * QC + 2])
    grad_c = [
        to_row(grads.at[:, slot(p), :], grad_out.at[:, row], grad_ss.at[n], grad_rs.at[n], p)
        for n, p in enumerate(peers)
    ]
    grad_own = pltpu.make_async_copy(grads.at[:, mine, :], grad_out.at[:, row], own_s.at[0, 2 * QC + 3])
    for c in mix_c + [mix_own] + grad_c + [grad_own]:
        c.start()

    tri_c = []
    wx_c = [
        to_grp(wo_all.at[:, :, sixth], wo_all.at[:, :, sixth], wx_ss.at[n], wx_rs.at[n], gpeers[n])
        for n in range(7)
    ]
    for q in range(QC):
        if q == QC - 1:

            @pl.when(fetches)
            def _():
                for c in wo_c + [wo_own]:
                    c.wait()
                for c in wx_c:
                    c.start()

        for c in left_c[q]:
            c.wait()
        for c in x_c[q]:
            c.wait()

        cuts = ((0, NB),) if q < QC - 1 else tuple((r * KS, KS) for r in range(BR))
        for h, (first, count) in enumerate(cuts):

            @pl.loop(first, first + count)
            def _(b):
                r = b // KS
                lhs, rhs = [], []
                for t in range(KS):
                    code = place[b * KS + t]
                    near = right[q][jnp.minimum(code, NB - 1)]
                    far = xr[q][jnp.clip(code - NB, 0, 55)]
                    block = jnp.where(code < NB, near, far)
                    rhs.append(jnp.where(code < NB + 56, block, jnp.zeros_like(block)))
                    lhs.append(left[q][r * KS + t])
                tri[q][b] = dot_nt(jnp.concatenate(lhs, axis=1), jnp.concatenate(rhs, axis=1)).astype(BF16)

            here = pl.ds(first, count)
            tri_c.append([
                to_row(tri[q].at[here, slot(p), :], tri_out.at[here, q, row], tri_ss.at[q + h, n], tri_rs.at[q + h, n], p)
                for n, p in enumerate(peers)
            ] + [pltpu.make_async_copy(tri[q].at[here, mine, :], tri_out.at[here, q, row], own_s.at[1, 8 + q + h])])
            start(tri_c[-1])

    for c in mix_c + [mix_own]:
        c.wait()

    @pl.when(fetches)
    def _():
        for c in wx_c:
            c.wait_send()

    for n, o in enumerate(GRP_ORDER):

        @pl.when((chip - o // 2 + 4) % 4 < 3)
        def _():
            wx_c[n].wait_recv()

    acc = nodes[rows32(row), :].astype(F32)
    for p in range(ROW):
        acc = acc + dot_nn(mixed_r[p, :, VOFF : VOFF + 48], wo_all[p])
    node_out[...] = acc.astype(BF16)

    for c in saves + grad_c + [grad_own]:
        c.wait()
    for part in tri_c:
        for c in part:
            c.wait()


def exchange(scalars, tensors, nodes):
    smem = pl.BlockSpec(memory_space=pltpu.SMEM)
    vmem = pl.BlockSpec(memory_space=pltpu.VMEM)
    anyspace = pl.BlockSpec(memory_space=pl.ANY)
    dma = pltpu.SemaphoreType.DMA
    blocks = lambda n: pltpu.VMEM((n, BLK, BLK), BF16)
    blocks_2d = pltpu.VMEM((BLK, BLK), BF16)
    n = ROW - 1
    scratch = (
        [blocks(NB)] * QC + [blocks(NB)] * QC + [blocks(NB)] * QC + [blocks(56)] * QC + [blocks(56)] * QC
        + [pltpu.VMEM((ROW, k, 8, BLK), BF16) for _, k in PARTS]
        + [pltpu.VMEM((CH - ROW, k, 8, BLK), BF16) for _, k in PARTS]
        + [pltpu.VMEM((CH, NB, 8, BLK), BF16), pltpu.VMEM((ROW, NB, 8, BLK), BF16)]
        + [pltpu.VMEM((k, 8, BLK, CZ), BF16) for _, k in PARTS]
        + [pltpu.VMEM((k, 8 * BLK, CZ), BF16) for _, k in PARTS]
        + [
            pltpu.VMEM((4 * CH + ROW, CZ), BF16), blocks_2d, pltpu.VMEM(((CH + ROW) * 8, BLK), F32),
            pltpu.VMEM((8 * BLK, CZ), F32), pltpu.VMEM((8 * BLK, CZ), F32), blocks_2d,
            pltpu.VMEM((2 * ROW, CZ), BF16), pltpu.VMEM((2 * (CH - ROW), CZ), BF16),
            pltpu.SMEM((NB * KS,), jnp.int32), pltpu.SMEM((NB,), jnp.int32),
            pltpu.SMEM((56,), jnp.int32), pltpu.SMEM((14,), jnp.int32),
        ]
        + [
            blocks(NB), blocks(NB), blocks(BR), blocks(14), blocks(14), blocks(BR + 14), blocks(BR), blocks(BR),
            pltpu.VMEM((BR * BLK, PAD), BF16), pltpu.VMEM((ROW, 32, PAD), BF16),
            pltpu.VMEM((ROW, 48, 768), BF16), pltpu.VMEM((PAD, 768), BF16), pltpu.VMEM((PAD, 768), BF16),
            pltpu.VMEM((PAD, 768), BF16), pltpu.VMEM((KS, BLK, BLK), F32), pltpu.VMEM((KS, BLK, BLK), F32),
        ]
        + [dma((len(PARTS) * QC, n))] * 2 + [dma((QC, n))] * 2 + [dma((QC - 1 + BR, n))] * 2 + [dma((QC, 7))] * 2 + [dma((7,))] * 2 + [dma((n,))] * 8
        + [dma((len(PARTS), 2 * QC + BR + QC)), dma((len(PARTS),)), dma((7,)), dma((7,)), dma((2, len(PARTS)))]
    )
    return pl.pallas_call(
        exchange_kernel,
        in_specs=[smem] * 4 + [anyspace] + [vmem] * 9,
        out_specs=[anyspace, anyspace, vmem, anyspace, anyspace, vmem],
        out_shape=[
            jax.ShapeDtypeStruct((NB, QC, ROW, 8, BLK), BF16),
            jax.ShapeDtypeStruct((NB, ROW, 8, BLK), BF16),
            jax.ShapeDtypeStruct((32, 768), BF16),
            jax.ShapeDtypeStruct((NB, 8 * BLK, CZ), BF16),
            jax.ShapeDtypeStruct((NB, 8, BLK, CZ), BF16),
            jax.ShapeDtypeStruct((NB, 8, BLK), F32),
        ],
        scratch_shapes=scratch,
        compiler_params=pltpu.CompilerParams(
            collective_id=0, has_side_effects=True, vmem_limit_bytes=63 << 20
        ),
        name="exchange",
    )(*scalars, *tensors, *nodes)


def finish_kernel(
    pair, tri, grads, normed, gate, scale, out_w, bias_w, pair_out, pair_grad,
    weights, ones, turned, hidden, both, along,
):
    @pl.when(pl.program_id(0) == 0)
    def _():
        bias = bias_w[...].astype(F32)
        weights[...] = jnp.zeros_like(weights)
        weights[:CH, :CZ] = out_w[...] * 0.5
        weights[CH : CH + ROW, CZ:] = (bias - jnp.mean(bias, axis=1, keepdims=True)).astype(BF16)
        ones[...] = jnp.full_like(ones, 1.0 / CZ)
        turned[...] = jnp.zeros_like(turned)

    def norm(k):
        sums = tri[k].astype(F32)
        centred = sums - jnp.mean(sums, axis=0, keepdims=True)
        spread = jnp.mean(centred * centred, axis=0, keepdims=True)
        turned[k, : 8 * CH] = (centred * lax.rsqrt(spread + EPS)).reshape(8 * CH, BLK)
        turned[k, 8 * CH : 8 * (CH + ROW)] = (grads[k].astype(F32) * scale[k]).reshape(8 * ROW, BLK)

    def turn(k):
        for i in range(8):
            hidden[k, i * BLK : (i + 1) * BLK, :] = turned[k, pl.ds(i, PAD, stride=8), :].astype(BF16).T

    def product(k):
        both[k] = dot_nn(hidden[k], weights[...])

    def project(k):
        along[k] = dot_nn(both[k, :, CZ:].astype(BF16) * normed[k], ones[...])

    def store(k):
        for i in range(8):
            rows = slice(i * BLK, (i + 1) * BLK)
            pair_out[k, i] = pair[k, i] + gate[k, i] * both[k, rows, :CZ].astype(BF16)
            pair_grad[k, i] = both[k, rows, CZ:].astype(BF16) - normed[k, rows, :] * along[k, rows, :].astype(BF16)

    norm(0)
    for k in range(STEP):
        turn(k)
        if k + 1 < STEP:
            norm(k + 1)
        product(k)
        if k > 0:
            store(k - 1)
        project(k)
    store(STEP - 1)


def finish(pair, tri, grads, normed, gate, scale, out_w, bias_w):
    by_block = lambda a: pl.BlockSpec((STEP,) + a.shape[1:], lambda b: (b,) + (0,) * (a.ndim - 1))
    whole = lambda a: pl.BlockSpec(a.shape, lambda b: (0,) * a.ndim)
    return pl.pallas_call(
        finish_kernel,
        grid=(NB // STEP,),
        in_specs=[by_block(a) for a in (pair, tri, grads, normed, gate, scale)] + [whole(out_w), whole(bias_w)],
        out_specs=[by_block(pair), by_block(pair)],
        out_shape=[jax.ShapeDtypeStruct(pair.shape, BF16)] * 2,
        scratch_shapes=[
            pltpu.VMEM((PAD, 2 * CZ), BF16),
            pltpu.VMEM((CZ, CZ), BF16),
            pltpu.VMEM((STEP, PAD * 8, BLK), F32),
            pltpu.VMEM((STEP, 8 * BLK, PAD), BF16),
            pltpu.VMEM((STEP, 8 * BLK, 2 * CZ), F32),
            pltpu.VMEM((STEP, 8 * BLK, CZ), F32),
        ],
        compiler_params=pltpu.CompilerParams(vmem_limit_bytes=62 << 20),
        name="finish",
    )(pair, tri, grads, normed, gate, scale, out_w, bias_w)


def per_device(
    pair_feats,
    block_cols,
    attn_mask,
    chain_of_row,
    same_chain,
    node_feats,
    node_cotangent,
    tri_weight,
    gate_weight,
    tri_out_weight,
    bias_weight,
    query_weight,
    key_weight,
    value_weight,
    out_weight,
):
    pair = pair_feats.reshape(NB, 8, BLK, CZ)
    bias_t = bias_weight.T
    tri, grads, node_out, normed, gate, scale = exchange(
        (block_cols.T, attn_mask.T, chain_of_row, same_chain),
        (pair, tri_weight, gate_weight, bias_t),
        (node_feats, node_cotangent, query_weight.T, key_weight.T, value_weight.T, out_weight),
    )
    pair_out, pair_grad = finish(
        pair, tri.reshape(NB, CH, 8, BLK), grads, normed, gate, scale, tri_out_weight, bias_t
    )
    return pair_out.reshape(pair_feats.shape), node_out, pair_grad.reshape(pair_feats.shape)


def solution(mesh):
    pair_spec = P("grp", None, "row", None, None)
    node_spec = P("grp", None)
    in_specs = (
        (pair_spec,) + (P(),) * 4 + (node_spec,) * 2 + (P(),) * 4 + (P(None, "row"),) * 3 + (P("row", None),)
    )
    out_specs = (pair_spec, P(("grp", "row"), None), pair_spec)
    return jax.shard_map(per_device, mesh=mesh, in_specs=in_specs, out_specs=out_specs, check_vma=False)
```

```python
import jax
import jax.numpy as jnp
from jax import lax
from jax.experimental import pallas as pl
from jax.experimental.pallas import tpu as pltpu
from jax.sharding import PartitionSpec as P

F32 = jnp.float32
BF16 = jnp.bfloat16
MESH = pl.DeviceIdType.MESH
EPS = 1e-5
GRP, ROW = 8, 16
BR, KS, BLK, CZ, CH = 4, 6, 128, 128, 64
NB = BR * KS
QC = CH // ROW
PAD = 128
STEP = 2
VOFF = 64
PARTS = ((0, 6), (6, 10), (16, 8))
ROW_ORDER = (1, 3, 4, 12, 2, 8, 5, 15, 7, 13, 6, 14, 9, 11, 10)
GRP_ORDER = (2, 6, 4, 3, 7, 5, 1)


def row_peer(row, offset):
    z, y = row // 4, row % 4
    return ((z + offset // 4) % 4) * 4 + (y + offset % 4) % 4


def grp_peer(grp, offset):
    x, core = grp // 2, grp % 2
    return ((x + offset // 2) % 4) * 2 + (core + offset % 2) % 2


def layer_norm(values):
    center = jnp.mean(values, axis=-1, keepdims=True)
    shifted = values - center
    spread = jnp.mean(shifted * shifted, axis=-1, keepdims=True)
    inverse = lax.rsqrt(spread + EPS)
    return shifted * inverse, inverse


def dot_nt(a, b):
    return lax.dot_general(a, b, (((1,), (1,)), ((), ())), preferred_element_type=F32)


def dot_nn(a, b):
    return lax.dot_general(a, b, (((1,), (0,)), ((), ())), preferred_element_type=F32)


def dot_tn(a, b):
    return lax.dot_general(a, b, (((0,), (0,)), ((), ())), preferred_element_type=F32)


def i32(flag):
    return jnp.where(flag, 1, 0).astype(jnp.int32)


def named_ranks(cols, reader, owner):
    flags = [jnp.int32(0)] * BR
    for r in range(BR):
        for s in range(KS):
            c = cols[s, reader * BR + r]
            for l in range(BR):
                flags[l] = flags[l] | i32(c == owner * BR + l)
    ranks, count = [], jnp.int32(0)
    firsts = [jnp.int32(0), jnp.int32(0)]
    for l in range(BR):
        ranks.append(count)
        for a in range(2):
            firsts[a] = firsts[a] + l * flags[l] * i32(count == a)
        count = count + flags[l]
    return ranks, firsts


def pick(entries, index):
    out = jnp.int32(0)
    for n, entry in enumerate(entries):
        out = out + entry * i32(index == n)
    return out


def write_places(cols, grp, step, place, kvplace):
    inner = step // KS
    slot = step % KS
    j = cols[slot, grp * BR + inner]
    owner = j >> 2
    own = owner == grp
    ranks, _ = named_ranks(cols, grp, owner)
    offset = ((grp // 2 - owner // 2 + 4) % 4) * 2 + (grp % 2 - owner % 2 + 2) % 2
    rank_j = pick(ranks, j & 3)
    theirs = [cols[u, j] for u in range(KS)]
    for t in range(KS):
        c = cols[t, grp * BR + inner]
        found, far, count = jnp.int32(-1), jnp.int32(0), jnp.int32(0)
        for u in range(KS):
            hit = theirs[u] == c
            found = jnp.where(hit, u, found)
            far = jnp.where(hit, count, far)
            count = count + i32((theirs[u] >> 2) != owner)
        n = jnp.where((c >> 2) == owner, pick(ranks, c & 3), 2 + far)
        remote = NB + (offset - 1) * 8 + rank_j * 4 + n
        place[step * KS + t] = jnp.where(
            found >= 0, jnp.where(own, (j & 3) * KS + found, remote), NB + 56
        )
    kvplace[step] = jnp.where(own, j & 3, BR + (offset - 1) * 2 + rank_j)


def write_stages(cols, grp, to, stage, kvstage):
    reader = grp_peer(grp, to)
    _, firsts = named_ranks(cols, reader, grp)
    for a in range(2):
        near, far = [jnp.int32(0)] * 2, [jnp.int32(0)] * 2
        count = jnp.int32(0)
        for u in range(KS):
            c = cols[u, grp * BR + firsts[a]]
            away = i32((c >> 2) != grp)
            for n in range(2):
                near[n] = near[n] + u * i32(c == grp * BR + firsts[n])
                far[n] = far[n] + u * away * i32(count == n)
            count = count + away
        for n in range(2):
            stage[(to - 1) * 8 + a * 4 + n] = firsts[a] * KS + near[n]
            stage[(to - 1) * 8 + a * 4 + 2 + n] = firsts[a] * KS + far[n]
        kvstage[(to - 1) * 2 + a] = firsts[a]


def exchange_kernel(*refs):
    (
        cols, mask, chain, same, pair, tri_w, gate_w, bias_w, nodes, cotan, q_w, k_w, v_w, o_w,
        tri_out, grad_out, node_out, normed_out, gate_out, scale_out,
    ) = refs[:20]
    scr = list(refs[20:])
    take = lambda n: [scr.pop(0) for _ in range(n)]
    right = take(QC)
    left = take(QC)
    tri = take(QC)
    xs = take(QC)
    xr = take(QC)
    first_s = take(len(PARTS))
    rest_s = take(len(PARTS))
    left_s, bias_s = take(2)
    pair_v = take(len(PARTS))
    normed_v = take(len(PARTS))
    weights, ones, turned, shifted, inverse, gates, first_w, rest_w, place, kvplace, stage, kvstage = take(12)
    (bias, grads, kv_own, kv_s, kv_r, kv_all, queries, cots, mixed, mixed_r, wo_all,
     wq_pad, wkv_pad, wo_pad, scores, gprobs) = take(16)
    (right_ss, right_rs, left_ss, left_rs, tri_ss, tri_rs, x_ss, x_rs,
     kv_ss, kv_rs, grad_ss, grad_rs, mix_ss, mix_rs, wo_ss, wo_rs, bias_ss, bias_rs, own_s, pair_s, wx_ss, wx_rs, save_s) = take(23)

    grp = lax.axis_index("grp")
    row = lax.axis_index("row")
    mine = pl.ds(pl.multiple_of(row * 8, 8), 8)

    def to_row(src, dst, ss, rs, peer):
        return pltpu.make_async_remote_copy(
            src, dst, ss, rs, device_id=(grp, peer), device_id_type=MESH
        )

    def to_grp(src, dst, ss, rs, peer):
        return pltpu.make_async_remote_copy(
            src, dst, ss, rs, device_id=(peer, row), device_id_type=MESH
        )

    loads = [
        pltpu.make_async_copy(pair.at[pl.ds(first, count)], pair_v[h], pair_s.at[h])
        for h, (first, count) in enumerate(PARTS)
    ]
    for c in loads:
        c.start()

    barrier = pltpu.get_barrier_semaphore()
    for offset in ROW_ORDER:
        pl.semaphore_signal(barrier, inc=1, device_id=(grp, row_peer(row, offset)), device_id_type=MESH)
    for offset in GRP_ORDER:
        pl.semaphore_signal(barrier, inc=1, device_id=(grp_peer(grp, offset), row), device_id_type=MESH)
    wo_pad[...] = jnp.zeros_like(wo_pad)
    weights[: 4 * CH, :] = (tri_w[...].astype(F32).T * 0.5).astype(BF16)
    weights[4 * CH :, :] = bias_w[...]
    ones[...] = jnp.full_like(ones, 1.0 / CZ)

    gates[...] = gate_w[...] * 0.5
    first_w[:ROW] = weights[2 * CH : 2 * CH + ROW]
    first_w[ROW:] = weights[3 * CH : 3 * CH + ROW]
    rest_w[: CH - ROW] = weights[2 * CH + ROW : 3 * CH]
    rest_w[CH - ROW :] = weights[3 * CH + ROW : 4 * CH]

    peers = [row_peer(row, offset) for offset in ROW_ORDER]

    def to_all(part, q, src, n_part):
        first, count = part
        here = pl.ds(first, count)
        return [
            to_row(src(p), right[q].at[here, mine, :], right_ss.at[n_part, n], right_rs.at[n_part, n], p)
            for n, p in enumerate(peers)
        ] + [pltpu.make_async_copy(src(row), right[q].at[here, mine, :], own_s.at[2, n_part])]

    right_c = [[to_all(part, 0, lambda p: first_s[h].at[p], h) for h, part in enumerate(PARTS)]] + [
        [
            to_all(part, q, lambda p: rest_s[h].at[(q - 1) * ROW + p], q * len(PARTS) + h)
            for h, part in enumerate(PARTS)
        ]
        for q in range(1, QC)
    ]
    left_c = [
        [
            to_row(left_s.at[q * ROW + p], left[q].at[:, mine, :], left_ss.at[q, n], left_rs.at[q, n], p)
            for n, p in enumerate(peers)
        ]
        + [pltpu.make_async_copy(left_s.at[q * ROW + row], left[q].at[:, mine, :], own_s.at[1, QC + q])]
        for q in range(QC)
    ]
    bias_c = [
        to_row(bias_s.at[p], bias.at[:, mine, :], bias_ss.at[n], bias_rs.at[n], p) for n, p in enumerate(peers)
    ] + [pltpu.make_async_copy(bias_s.at[row], bias.at[:, mine, :], own_s.at[0, 2 * QC])]
    chip = grp // 2
    fetches = chip < 3
    sixth = pl.ds(pl.multiple_of(lax.rem(grp, 6) * BLK, BLK), BLK)
    wo_c = [
        to_row(o_w.at[:, sixth], wo_all.at[row, :, sixth], wo_ss.at[n], wo_rs.at[n], p)
        for n, p in enumerate(peers)
    ]
    wo_own = pltpu.make_async_copy(o_w.at[:, sixth], wo_all.at[row, :, sixth], own_s.at[0, 2 * QC + 1])

    def start(copies):
        for c in copies:
            c.start()

    for h, (first, count) in enumerate(PARTS):
        loads[h].wait()

        @pl.loop(0, count)
        def _(b):
            values = pair_v[h][b].reshape(8 * BLK, CZ)
            inverse[...] = dot_nn(values, ones[...])
            shifted[...] = values.astype(F32) - inverse[...]
            inverse[...] = dot_nn((shifted[...] * shifted[...]).astype(BF16), ones[...])
            normed_v[h][b] = (shifted[...] * lax.rsqrt(inverse[...] + EPS)).astype(BF16)
            for i in range(8):
                normed = normed_v[h][b, i * BLK : (i + 1) * BLK, :]
                projected = dot_nt(first_w[...], normed)
                turned[pl.ds(i, ROW, stride=8), :] = (jnp.tanh(projected[ROW:]) + 1.0) * projected[:ROW]
            first_s[h][:, b] = turned[: 8 * ROW].reshape(ROW, 8, BLK).astype(BF16)

        if h == 0:
            pl.semaphore_wait(barrier, 22)
        start(right_c[0][h])

    def project_rest(h):
        first, count = PARTS[h]

        @pl.loop(0, count)
        def _(b):
            for i in range(8):
                normed = normed_v[h][b, i * BLK : (i + 1) * BLK, :]
                projected = dot_nt(rest_w[...], normed)
                turned[pl.ds(i, CH - ROW, stride=8), :] = (
                    jnp.tanh(projected[CH - ROW :]) + 1.0
                ) * projected[: CH - ROW]
            rest_s[h][:, b] = turned[: 8 * (CH - ROW)].reshape(CH - ROW, 8, BLK).astype(BF16)

        for q in range(1, QC):
            start(right_c[q][h])

    project_rest(0)

    @pl.loop(1, GRP)
    def _(to):
        write_stages(cols, grp, to, stage, kvstage)

    saves = [
        pltpu.make_async_copy(normed_v[h], normed_out.at[pl.ds(first, count)], save_s.at[0, h])
        for h, (first, count) in enumerate(PARTS)
    ]
    start(saves)

    gpeers = [grp_peer(grp, offset) for offset in GRP_ORDER]
    x_c = []

    def exchange_channel(q):
        for part in right_c[q]:
            for c in part:
                c.wait()

        @pl.loop(0, 56)
        def _(n):
            xs[q][n] = right[q][stage[n]]

        x_c.append([
            to_grp(
                xs[q].at[pl.ds((o - 1) * 8, 8)], xr[q].at[pl.ds((o - 1) * 8, 8)],
                x_ss.at[q, n], x_rs.at[q, n], gpeers[n],
            )
            for n, o in enumerate(GRP_ORDER)
        ])
        start(x_c[q])

    exchange_channel(0)
    for h in range(1, len(PARTS)):
        project_rest(h)

    wq_pad[...] = jnp.zeros_like(wq_pad)
    wkv_pad[...] = jnp.zeros_like(wkv_pad)
    wq_pad[:48, :] = q_w[...]
    wkv_pad[:48, :] = k_w[...]
    wkv_pad[VOFF : VOFF + 48, :] = v_w[...]
    wo_pad[VOFF : VOFF + 48, :] = o_w[...]

    @pl.loop(0, BR)
    def _(r):
        part = pl.ds(pl.multiple_of(r * BLK, BLK), BLK)
        normed = layer_norm(nodes[part, :].astype(F32))[0].astype(BF16)
        queries[r] = dot_nt(normed, wq_pad[...]).astype(BF16)
        kv_own[r] = dot_nt(normed, wkv_pad[...]).astype(BF16)
        cots[r] = dot_nt(cotan[part, :], wo_pad[...]).astype(BF16)

    for n in range(14):
        kv_s[n] = kv_own[kvstage[n]]
    kv_c = [
        to_grp(kv_s.at[pl.ds((o - 1) * 2, 2)], kv_r.at[pl.ds((o - 1) * 2, 2)], kv_ss.at[n], kv_rs.at[n], gpeers[n])
        for n, o in enumerate(GRP_ORDER)
    ]
    start(kv_c)

    for h, (first, count) in enumerate(PARTS):

        @pl.loop(0, count)
        def _(b):
            for i in range(8):
                normed = normed_v[h][b, i * BLK : (i + 1) * BLK, :]
                projected = dot_nt(weights[: 2 * CH, :], normed)
                turned[pl.ds(i, CH, stride=8), :] = (jnp.tanh(projected[CH:]) + 1.0) * projected[:CH]
                turned[pl.ds(8 * CH + i, ROW, stride=8), :] = dot_nt(weights[4 * CH :, :], normed)
            left_s[:, first + b] = turned[: 8 * CH].reshape(CH, 8, BLK).astype(BF16)
            bias_s[:, first + b] = turned[8 * CH :].reshape(ROW, 8, BLK).astype(BF16)

    start(bias_c)
    for q in range(QC):
        start(left_c[q])

    @pl.when(fetches)
    def _():
        start(wo_c + [wo_own])

    exchange_channel(1)

    for h, (first, count) in enumerate(PARTS):

        @pl.loop(0, count)
        def _(b):
            values = pair_v[h][b].reshape(8 * BLK, CZ)
            shifted[...] = values.astype(F32) - dot_nn(values, ones[...])
            squares = (shifted[...] * shifted[...]).astype(BF16)
            for i in range(8):
                spread = dot_nt(ones[:8], squares[i * BLK : (i + 1) * BLK])
                scale_out[first + b, i : i + 1, :] = lax.rsqrt(spread[:1] + EPS)
            inverse[...] = jnp.tanh(dot_nn(normed_v[h][b], gates[...])) + 1.0
            pair_v[h][b] = inverse[...].astype(BF16).reshape(8, BLK, CZ)

        saves.append(pltpu.make_async_copy(pair_v[h], gate_out.at[pl.ds(first, count)], save_s.at[1, h]))
        saves[-1].start()

    exchange_channel(2)
    exchange_channel(3)

    @pl.loop(0, NB)
    def _(b):
        write_places(cols, grp, b, place, kvplace)

    for c in kv_c:
        c.wait()
    for c in bias_c:
        c.wait()
    kv_all[:BR] = kv_own[...]
    kv_all[BR:] = kv_r[...]
    chain_bias = same[row]

    @pl.loop(0, BR)
    def _(r):
        here = chain[grp * BR + r]
        query = queries[r]
        cot = cots[r]
        top = jnp.full((BLK, 1), -jnp.inf, F32)
        for s in range(KS):
            kv = kv_all[kvplace[r * KS + s]]
            j = cols[s, grp * BR + r]
            extra = jnp.where(chain[j] == here, chain_bias, 0.0)
            part = dot_nt(query, kv) * (48 ** -0.5) + (bias[r * KS + s].astype(F32) + extra)
            part = jnp.where(mask[s, grp * BR + r] > 0, part, -jnp.inf)
            scores[s] = part
            gprobs[s] = dot_nt(cot, kv)
            top = jnp.maximum(top, jnp.max(part, axis=1, keepdims=True))
        total = jnp.zeros((BLK, 1), F32)
        for s in range(KS):
            part = jnp.exp(scores[s] - top)
            scores[s] = part
            total = total + jnp.sum(part, axis=1, keepdims=True)
        inverse = 1.0 / total
        dots = jnp.zeros((BLK, 1), F32)
        mix = jnp.zeros((BLK, PAD), F32)
        for s in range(KS):
            probs = scores[s] * inverse
            scores[s] = probs
            dots = dots + jnp.sum(probs * gprobs[s], axis=1, keepdims=True)
            mix = mix + dot_nn(probs.astype(BF16), kv_all[kvplace[r * KS + s]])
        for s in range(KS):
            grads[r * KS + s] = (scores[s] * (gprobs[s] - dots)).astype(BF16)
        mixed[pl.ds(pl.multiple_of(r * BLK, BLK), BLK), :] = mix.astype(BF16)

    slot = lambda p: pl.ds(pl.multiple_of(p * 8, 8), 8)
    rows32 = lambda p: pl.ds(pl.multiple_of(p * 32, 32), 32)
    mix_c = [
        to_row(mixed.at[rows32(p)], mixed_r.at[row], mix_ss.at[n], mix_rs.at[n], p) for n, p in enumerate(peers)
    ]
    mix_own = pltpu.make_async_copy(mixed.at[rows32(row)], mixed_r.at[row], own_s.at[0, 2 * QC + 2])
    grad_c = [
        to_row(grads.at[:, slot(p), :], grad_out.at[:, row], grad_ss.at[n], grad_rs.at[n], p)
        for n, p in enumerate(peers)
    ]
    grad_own = pltpu.make_async_copy(grads.at[:, mine, :], grad_out.at[:, row], own_s.at[0, 2 * QC + 3])
    for c in mix_c + [mix_own] + grad_c + [grad_own]:
        c.start()

    tri_c = []
    wx_c = [
        to_grp(wo_all.at[:, :, sixth], wo_all.at[:, :, sixth], wx_ss.at[n], wx_rs.at[n], gpeers[n])
        for n in range(7)
    ]
    for q in range(QC):
        if q == QC - 1:

            @pl.when(fetches)
            def _():
                for c in wo_c + [wo_own]:
                    c.wait()
                for c in wx_c:
                    c.start()

        for c in left_c[q]:
            c.wait()
        for c in x_c[q]:
            c.wait()

        cuts = ((0, NB),) if q < QC - 1 else ((0, NB // 2), (NB // 2, NB // 2))
        for h, (first, count) in enumerate(cuts):

            @pl.loop(first, first + count)
            def _(b):
                r = b // KS
                lhs, rhs = [], []
                for t in range(KS):
                    code = place[b * KS + t]
                    near = right[q][jnp.minimum(code, NB - 1)]
                    far = xr[q][jnp.clip(code - NB, 0, 55)]
                    block = jnp.where(code < NB, near, far)
                    rhs.append(jnp.where(code < NB + 56, block, jnp.zeros_like(block)))
                    lhs.append(left[q][r * KS + t])
                tri[q][b] = dot_nt(jnp.concatenate(lhs, axis=1), jnp.concatenate(rhs, axis=1)).astype(BF16)

            here = pl.ds(first, count)
            tri_c.append([
                to_row(tri[q].at[here, slot(p), :], tri_out.at[here, q, row], tri_ss.at[q + h, n], tri_rs.at[q + h, n], p)
                for n, p in enumerate(peers)
            ] + [pltpu.make_async_copy(tri[q].at[here, mine, :], tri_out.at[here, q, row], own_s.at[1, 8 + q + h])])
            start(tri_c[-1])

    for c in mix_c + [mix_own]:
        c.wait()

    @pl.when(fetches)
    def _():
        for c in wx_c:
            c.wait_send()

    for n, o in enumerate(GRP_ORDER):

        @pl.when((chip - o // 2 + 4) % 4 < 3)
        def _():
            wx_c[n].wait_recv()

    acc = nodes[rows32(row), :].astype(F32)
    for p in range(ROW):
        acc = acc + dot_nn(mixed_r[p, :, VOFF : VOFF + 48], wo_all[p])
    node_out[...] = acc.astype(BF16)

    for c in saves + grad_c + [grad_own]:
        c.wait()
    for part in tri_c:
        for c in part:
            c.wait()


def exchange(scalars, tensors, nodes):
    smem = pl.BlockSpec(memory_space=pltpu.SMEM)
    vmem = pl.BlockSpec(memory_space=pltpu.VMEM)
    anyspace = pl.BlockSpec(memory_space=pl.ANY)
    dma = pltpu.SemaphoreType.DMA
    blocks = lambda n: pltpu.VMEM((n, BLK, BLK), BF16)
    blocks_2d = pltpu.VMEM((BLK, BLK), BF16)
    n = ROW - 1
    scratch = (
        [blocks(NB)] * QC + [blocks(NB)] * QC + [blocks(NB)] * QC + [blocks(56)] * QC + [blocks(56)] * QC
        + [pltpu.VMEM((ROW, k, 8, BLK), BF16) for _, k in PARTS]
        + [pltpu.VMEM((CH - ROW, k, 8, BLK), BF16) for _, k in PARTS]
        + [pltpu.VMEM((CH, NB, 8, BLK), BF16), pltpu.VMEM((ROW, NB, 8, BLK), BF16)]
        + [pltpu.VMEM((k, 8, BLK, CZ), BF16) for _, k in PARTS]
        + [pltpu.VMEM((k, 8 * BLK, CZ), BF16) for _, k in PARTS]
        + [
            pltpu.VMEM((4 * CH + ROW, CZ), BF16), blocks_2d, pltpu.VMEM(((CH + ROW) * 8, BLK), F32),
            pltpu.VMEM((8 * BLK, CZ), F32), pltpu.VMEM((8 * BLK, CZ), F32), blocks_2d,
            pltpu.VMEM((2 * ROW, CZ), BF16), pltpu.VMEM((2 * (CH - ROW), CZ), BF16),
            pltpu.SMEM((NB * KS,), jnp.int32), pltpu.SMEM((NB,), jnp.int32),
            pltpu.SMEM((56,), jnp.int32), pltpu.SMEM((14,), jnp.int32),
        ]
        + [
            blocks(NB), blocks(NB), blocks(BR), blocks(14), blocks(14), blocks(BR + 14), blocks(BR), blocks(BR),
            pltpu.VMEM((BR * BLK, PAD), BF16), pltpu.VMEM((ROW, 32, PAD), BF16),
            pltpu.VMEM((ROW, 48, 768), BF16), pltpu.VMEM((PAD, 768), BF16), pltpu.VMEM((PAD, 768), BF16),
            pltpu.VMEM((PAD, 768), BF16), pltpu.VMEM((KS, BLK, BLK), F32), pltpu.VMEM((KS, BLK, BLK), F32),
        ]
        + [dma((len(PARTS) * QC, n))] * 2 + [dma((QC, n))] * 2 + [dma((QC + 1, n))] * 2 + [dma((QC, 7))] * 2 + [dma((7,))] * 2 + [dma((n,))] * 8
        + [dma((len(PARTS), 2 * QC + 1 + QC)), dma((len(PARTS),)), dma((7,)), dma((7,)), dma((2, len(PARTS)))]
    )
    return pl.pallas_call(
        exchange_kernel,
        in_specs=[smem] * 4 + [anyspace] + [vmem] * 9,
        out_specs=[anyspace, anyspace, vmem, anyspace, anyspace, vmem],
        out_shape=[
            jax.ShapeDtypeStruct((NB, QC, ROW, 8, BLK), BF16),
            jax.ShapeDtypeStruct((NB, ROW, 8, BLK), BF16),
            jax.ShapeDtypeStruct((32, 768), BF16),
            jax.ShapeDtypeStruct((NB, 8 * BLK, CZ), BF16),
            jax.ShapeDtypeStruct((NB, 8, BLK, CZ), BF16),
            jax.ShapeDtypeStruct((NB, 8, BLK), F32),
        ],
        scratch_shapes=scratch,
        compiler_params=pltpu.CompilerParams(
            collective_id=0, has_side_effects=True, vmem_limit_bytes=56<<20
        ),
        name="exchange",
    )(*scalars, *tensors, *nodes)


def finish_kernel(
    pair, tri, grads, normed, gate, scale, out_w, bias_w, pair_out, pair_grad,
    weights, ones, turned, hidden, both, along,
):
    @pl.when(pl.program_id(0) == 0)
    def _():
        bias = bias_w[...].astype(F32)
        weights[...] = jnp.zeros_like(weights)
        weights[:CH, :CZ] = out_w[...] * 0.5
        weights[CH : CH + ROW, CZ:] = (bias - jnp.mean(bias, axis=1, keepdims=True)).astype(BF16)
        ones[...] = jnp.full_like(ones, 1.0 / CZ)
        turned[...] = jnp.zeros_like(turned)

    def norm(k):
        sums = tri[k].astype(F32)
        centred = sums - jnp.mean(sums, axis=0, keepdims=True)
        spread = jnp.mean(centred * centred, axis=0, keepdims=True)
        turned[k, : 8 * CH] = (centred * lax.rsqrt(spread + EPS)).reshape(8 * CH, BLK)
        turned[k, 8 * CH : 8 * (CH + ROW)] = (grads[k].astype(F32) * scale[k]).reshape(8 * ROW, BLK)

    def turn(k):
        for i in range(8):
            hidden[k, i * BLK : (i + 1) * BLK, :] = turned[k, pl.ds(i, PAD, stride=8), :].astype(BF16).T

    def product(k):
        both[k] = dot_nn(hidden[k], weights[...])

    def project(k):
        along[k] = dot_nn(both[k, :, CZ:].astype(BF16) * normed[k], ones[...])

    def store(k):
        for i in range(8):
            rows = slice(i * BLK, (i + 1) * BLK)
            pair_out[k, i] = pair[k, i] + gate[k, i] * both[k, rows, :CZ].astype(BF16)
            pair_grad[k, i] = both[k, rows, CZ:].astype(BF16) - normed[k, rows, :] * along[k, rows, :].astype(BF16)

    norm(0)
    for k in range(STEP):
        turn(k)
        if k + 1 < STEP:
            norm(k + 1)
        product(k)
        if k > 0:
            store(k - 1)
        project(k)
    store(STEP - 1)


def finish(pair, tri, grads, normed, gate, scale, out_w, bias_w):
    by_block = lambda a: pl.BlockSpec((STEP,) + a.shape[1:], lambda b: (b,) + (0,) * (a.ndim - 1))
    whole = lambda a: pl.BlockSpec(a.shape, lambda b: (0,) * a.ndim)
    return pl.pallas_call(
        finish_kernel,
        grid=(NB // STEP,),
        in_specs=[by_block(a) for a in (pair, tri, grads, normed, gate, scale)] + [whole(out_w), whole(bias_w)],
        out_specs=[by_block(pair), by_block(pair)],
        out_shape=[jax.ShapeDtypeStruct(pair.shape, BF16)] * 2,
        scratch_shapes=[
            pltpu.VMEM((PAD, 2 * CZ), BF16),
            pltpu.VMEM((CZ, CZ), BF16),
            pltpu.VMEM((STEP, PAD * 8, BLK), F32),
            pltpu.VMEM((STEP, 8 * BLK, PAD), BF16),
            pltpu.VMEM((STEP, 8 * BLK, 2 * CZ), F32),
            pltpu.VMEM((STEP, 8 * BLK, CZ), F32),
        ],
        compiler_params=pltpu.CompilerParams(vmem_limit_bytes=42<<20),
        name="finish",
    )(pair, tri, grads, normed, gate, scale, out_w, bias_w)


def per_device(
    pair_feats,
    block_cols,
    attn_mask,
    chain_of_row,
    same_chain,
    node_feats,
    node_cotangent,
    tri_weight,
    gate_weight,
    tri_out_weight,
    bias_weight,
    query_weight,
    key_weight,
    value_weight,
    out_weight,
):
    pair = pair_feats.reshape(NB, 8, BLK, CZ)
    bias_t = bias_weight.T
    tri, grads, node_out, normed, gate, scale = exchange(
        (block_cols.T, attn_mask.T, chain_of_row, same_chain),
        (pair, tri_weight, gate_weight, bias_t),
        (node_feats, node_cotangent, query_weight.T, key_weight.T, value_weight.T, out_weight),
    )
    pair_out, pair_grad = finish(
        pair, tri.reshape(NB, CH, 8, BLK), grads, normed, gate, scale, tri_out_weight, bias_t
    )
    return pair_out.reshape(pair_feats.shape), node_out, pair_grad.reshape(pair_feats.shape)


def solution(mesh):
    pair_spec = P("grp", None, "row", None, None)
    node_spec = P("grp", None)
    in_specs = (
        (pair_spec,) + (P(),) * 4 + (node_spec,) * 2 + (P(),) * 4 + (P(None, "row"),) * 3 + (P("row", None),)
    )
    out_specs = (pair_spec, P(("grp", "row"), None), pair_spec)
    return jax.shard_map(per_device, mesh=mesh, in_specs=in_specs, out_specs=out_specs, check_vma=False)
```

```python
import jax
import jax.numpy as jnp
from jax import lax
from jax.experimental import pallas as pl
from jax.experimental.pallas import tpu as pltpu
from jax.sharding import PartitionSpec as P

F32 = jnp.float32
BF16 = jnp.bfloat16
MESH = pl.DeviceIdType.MESH
EPS = 1e-5
GRP, ROW = 8, 16
BR, KS, BLK, CZ, CH = 4, 6, 128, 128, 64
NB = BR * KS
QC = CH // ROW
PAD = 128
STEP = 2
VOFF = 64
PARTS = ((0, 6), (6, 10), (16, 8))
ROW_ORDER = (1, 3, 4, 12, 2, 8, 5, 15, 7, 13, 6, 14, 9, 11, 10)
GRP_ORDER = (2, 6, 4, 3, 7, 5, 1)


def row_peer(row, offset):
    z, y = row // 4, row % 4
    return ((z + offset // 4) % 4) * 4 + (y + offset % 4) % 4


def grp_peer(grp, offset):
    x, core = grp // 2, grp % 2
    return ((x + offset // 2) % 4) * 2 + (core + offset % 2) % 2


def layer_norm(values):
    center = jnp.mean(values, axis=-1, keepdims=True)
    shifted = values - center
    spread = jnp.mean(shifted * shifted, axis=-1, keepdims=True)
    inverse = lax.rsqrt(spread + EPS)
    return shifted * inverse, inverse


def dot_nt(a, b):
    return lax.dot_general(a, b, (((1,), (1,)), ((), ())), preferred_element_type=F32)


def dot_nn(a, b):
    return lax.dot_general(a, b, (((1,), (0,)), ((), ())), preferred_element_type=F32)


def dot_tn(a, b):
    return lax.dot_general(a, b, (((0,), (0,)), ((), ())), preferred_element_type=F32)


def i32(flag):
    return jnp.where(flag, 1, 0).astype(jnp.int32)


def named_ranks(cols, reader, owner):
    flags = [jnp.int32(0)] * BR
    for r in range(BR):
        for s in range(KS):
            c = cols[s, reader * BR + r]
            for l in range(BR):
                flags[l] = flags[l] | i32(c == owner * BR + l)
    ranks, count = [], jnp.int32(0)
    firsts = [jnp.int32(0), jnp.int32(0)]
    for l in range(BR):
        ranks.append(count)
        for a in range(2):
            firsts[a] = firsts[a] + l * flags[l] * i32(count == a)
        count = count + flags[l]
    return ranks, firsts


def pick(entries, index):
    out = jnp.int32(0)
    for n, entry in enumerate(entries):
        out = out + entry * i32(index == n)
    return out


def write_places(cols, grp, step, place, kvplace):
    inner = step // KS
    slot = step % KS
    j = cols[slot, grp * BR + inner]
    owner = j >> 2
    own = owner == grp
    ranks, _ = named_ranks(cols, grp, owner)
    offset = ((grp // 2 - owner // 2 + 4) % 4) * 2 + (grp % 2 - owner % 2 + 2) % 2
    rank_j = pick(ranks, j & 3)
    theirs = [cols[u, j] for u in range(KS)]
    for t in range(KS):
        c = cols[t, grp * BR + inner]
        found, far, count = jnp.int32(-1), jnp.int32(0), jnp.int32(0)
        for u in range(KS):
            hit = theirs[u] == c
            found = jnp.where(hit, u, found)
            far = jnp.where(hit, count, far)
            count = count + i32((theirs[u] >> 2) != owner)
        n = jnp.where((c >> 2) == owner, pick(ranks, c & 3), 2 + far)
        remote = NB + (offset - 1) * 8 + rank_j * 4 + n
        place[step * KS + t] = jnp.where(
            found >= 0, jnp.where(own, (j & 3) * KS + found, remote), NB + 56
        )
    kvplace[step] = jnp.where(own, j & 3, BR + (offset - 1) * 2 + rank_j)


def write_stages(cols, grp, to, stage, kvstage):
    reader = grp_peer(grp, to)
    _, firsts = named_ranks(cols, reader, grp)
    for a in range(2):
        near, far = [jnp.int32(0)] * 2, [jnp.int32(0)] * 2
        count = jnp.int32(0)
        for u in range(KS):
            c = cols[u, grp * BR + firsts[a]]
            away = i32((c >> 2) != grp)
            for n in range(2):
                near[n] = near[n] + u * i32(c == grp * BR + firsts[n])
                far[n] = far[n] + u * away * i32(count == n)
            count = count + away
        for n in range(2):
            stage[(to - 1) * 8 + a * 4 + n] = firsts[a] * KS + near[n]
            stage[(to - 1) * 8 + a * 4 + 2 + n] = firsts[a] * KS + far[n]
        kvstage[(to - 1) * 2 + a] = firsts[a]


def exchange_kernel(*refs):
    (
        cols, mask, chain, same, pair, tri_w, gate_w, bias_w, nodes, cotan, q_w, k_w, v_w, o_w,
        tri_out, grad_out, node_out, normed_out, gate_out, scale_out,
    ) = refs[:20]
    scr = list(refs[20:])
    take = lambda n: [scr.pop(0) for _ in range(n)]
    right = take(QC)
    left = take(QC)
    tri = take(QC)
    xs = take(QC)
    xr = take(QC)
    first_s = take(len(PARTS))
    rest_s = take(len(PARTS))
    left_s, bias_s = take(2)
    pair_v = take(len(PARTS))
    normed_v = take(len(PARTS))
    weights, ones, turned, shifted, inverse, gates, first_w, rest_w, place, kvplace, stage, kvstage = take(12)
    (bias, grads, kv_own, kv_s, kv_r, kv_all, queries, cots, mixed, mixed_r, wo_all,
     wq_pad, wkv_pad, wo_pad, scores, gprobs) = take(16)
    (right_ss, right_rs, left_ss, left_rs, tri_ss, tri_rs, x_ss, x_rs,
     kv_ss, kv_rs, grad_ss, grad_rs, mix_ss, mix_rs, wo_ss, wo_rs, bias_ss, bias_rs, own_s, pair_s, wx_ss, wx_rs, save_s) = take(23)

    grp = lax.axis_index("grp")
    row = lax.axis_index("row")
    mine = pl.ds(pl.multiple_of(row * 8, 8), 8)

    def to_row(src, dst, ss, rs, peer):
        return pltpu.make_async_remote_copy(
            src, dst, ss, rs, device_id=(grp, peer), device_id_type=MESH
        )

    def to_grp(src, dst, ss, rs, peer):
        return pltpu.make_async_remote_copy(
            src, dst, ss, rs, device_id=(peer, row), device_id_type=MESH
        )

    loads = [
        pltpu.make_async_copy(pair.at[pl.ds(first, count)], pair_v[h], pair_s.at[h])
        for h, (first, count) in enumerate(PARTS)
    ]
    for c in loads:
        c.start()

    barrier = pltpu.get_barrier_semaphore()
    for offset in ROW_ORDER:
        pl.semaphore_signal(barrier, inc=1, device_id=(grp, row_peer(row, offset)), device_id_type=MESH)
    for offset in GRP_ORDER:
        pl.semaphore_signal(barrier, inc=1, device_id=(grp_peer(grp, offset), row), device_id_type=MESH)
    wo_pad[...] = jnp.zeros_like(wo_pad)
    weights[: 4 * CH, :] = (tri_w[...].astype(F32).T * 0.5).astype(BF16)
    weights[4 * CH :, :] = bias_w[...]
    ones[...] = jnp.full_like(ones, 1.0 / CZ)

    gates[...] = gate_w[...] * 0.5
    first_w[:ROW] = weights[2 * CH : 2 * CH + ROW]
    first_w[ROW:] = weights[3 * CH : 3 * CH + ROW]
    rest_w[: CH - ROW] = weights[2 * CH + ROW : 3 * CH]
    rest_w[CH - ROW :] = weights[3 * CH + ROW : 4 * CH]

    peers = [row_peer(row, offset) for offset in ROW_ORDER]

    def to_all(part, q, src, n_part):
        first, count = part
        here = pl.ds(first, count)
        return [
            to_row(src(p), right[q].at[here, mine, :], right_ss.at[n_part, n], right_rs.at[n_part, n], p)
            for n, p in enumerate(peers)
        ] + [pltpu.make_async_copy(src(row), right[q].at[here, mine, :], own_s.at[2, n_part])]

    right_c = [[to_all(part, 0, lambda p: first_s[h].at[p], h) for h, part in enumerate(PARTS)]] + [
        [
            to_all(part, q, lambda p: rest_s[h].at[(q - 1) * ROW + p], q * len(PARTS) + h)
            for h, part in enumerate(PARTS)
        ]
        for q in range(1, QC)
    ]
    left_c = [
        [
            to_row(left_s.at[q * ROW + p], left[q].at[:, mine, :], left_ss.at[q, n], left_rs.at[q, n], p)
            for n, p in enumerate(peers)
        ]
        + [pltpu.make_async_copy(left_s.at[q * ROW + row], left[q].at[:, mine, :], own_s.at[1, QC + q])]
        for q in range(QC)
    ]
    bias_c = [
        to_row(bias_s.at[p], bias.at[:, mine, :], bias_ss.at[n], bias_rs.at[n], p) for n, p in enumerate(peers)
    ] + [pltpu.make_async_copy(bias_s.at[row], bias.at[:, mine, :], own_s.at[0, 2 * QC])]
    chip = grp // 2
    fetches = chip < 3
    sixth = pl.ds(pl.multiple_of(lax.rem(grp, 6) * BLK, BLK), BLK)
    wo_c = [
        to_row(o_w.at[:, sixth], wo_all.at[row, :, sixth], wo_ss.at[n], wo_rs.at[n], p)
        for n, p in enumerate(peers)
    ]
    wo_own = pltpu.make_async_copy(o_w.at[:, sixth], wo_all.at[row, :, sixth], own_s.at[0, 2 * QC + 1])

    def start(copies):
        for c in copies:
            c.start()

    for h, (first, count) in enumerate(PARTS):
        loads[h].wait()

        @pl.loop(0, count)
        def _(b):
            values = pair_v[h][b].reshape(8 * BLK, CZ)
            inverse[...] = dot_nn(values, ones[...])
            shifted[...] = values.astype(F32) - inverse[...]
            inverse[...] = dot_nn((shifted[...] * shifted[...]).astype(BF16), ones[...])
            normed_v[h][b] = (shifted[...] * lax.rsqrt(inverse[...] + EPS)).astype(BF16)
            for i in range(8):
                normed = normed_v[h][b, i * BLK : (i + 1) * BLK, :]
                projected = dot_nt(first_w[...], normed)
                turned[pl.ds(i, ROW, stride=8), :] = (jnp.tanh(projected[ROW:]) + 1.0) * projected[:ROW]
            first_s[h][:, b] = turned[: 8 * ROW].reshape(ROW, 8, BLK).astype(BF16)

        if h == 0:
            pl.semaphore_wait(barrier, 22)
        start(right_c[0][h])

    def project_rest(h):
        first, count = PARTS[h]

        @pl.loop(0, count)
        def _(b):
            for i in range(8):
                normed = normed_v[h][b, i * BLK : (i + 1) * BLK, :]
                projected = dot_nt(rest_w[...], normed)
                turned[pl.ds(i, CH - ROW, stride=8), :] = (
                    jnp.tanh(projected[CH - ROW :]) + 1.0
                ) * projected[: CH - ROW]
            rest_s[h][:, b] = turned[: 8 * (CH - ROW)].reshape(CH - ROW, 8, BLK).astype(BF16)

        for q in range(1, QC):
            start(right_c[q][h])

    project_rest(0)

    @pl.loop(1, GRP)
    def _(to):
        write_stages(cols, grp, to, stage, kvstage)

    saves = [
        pltpu.make_async_copy(normed_v[h], normed_out.at[pl.ds(first, count)], save_s.at[0, h])
        for h, (first, count) in enumerate(PARTS)
    ]
    start(saves)

    gpeers = [grp_peer(grp, offset) for offset in GRP_ORDER]
    x_c = []

    def exchange_channel(q):
        for part in right_c[q]:
            for c in part:
                c.wait()

        @pl.loop(0, 56)
        def _(n):
            xs[q][n] = right[q][stage[n]]

        x_c.append([
            to_grp(
                xs[q].at[pl.ds((o - 1) * 8, 8)], xr[q].at[pl.ds((o - 1) * 8, 8)],
                x_ss.at[q, n], x_rs.at[q, n], gpeers[n],
            )
            for n, o in enumerate(GRP_ORDER)
        ])
        start(x_c[q])

    exchange_channel(0)
    for h in range(1, len(PARTS)):
        project_rest(h)

    wq_pad[...] = jnp.zeros_like(wq_pad)
    wkv_pad[...] = jnp.zeros_like(wkv_pad)
    wq_pad[:48, :] = q_w[...]
    wkv_pad[:48, :] = k_w[...]
    wkv_pad[VOFF : VOFF + 48, :] = v_w[...]
    wo_pad[VOFF : VOFF + 48, :] = o_w[...]

    @pl.loop(0, BR)
    def _(r):
        part = pl.ds(pl.multiple_of(r * BLK, BLK), BLK)
        normed = layer_norm(nodes[part, :].astype(F32))[0].astype(BF16)
        queries[r] = dot_nt(normed, wq_pad[...]).astype(BF16)
        kv_own[r] = dot_nt(normed, wkv_pad[...]).astype(BF16)
        cots[r] = dot_nt(cotan[part, :], wo_pad[...]).astype(BF16)

    for n in range(14):
        kv_s[n] = kv_own[kvstage[n]]
    kv_c = [
        to_grp(kv_s.at[pl.ds((o - 1) * 2, 2)], kv_r.at[pl.ds((o - 1) * 2, 2)], kv_ss.at[n], kv_rs.at[n], gpeers[n])
        for n, o in enumerate(GRP_ORDER)
    ]
    start(kv_c)

    for h, (first, count) in enumerate(PARTS):

        @pl.loop(0, count)
        def _(b):
            for i in range(8):
                normed = normed_v[h][b, i * BLK : (i + 1) * BLK, :]
                projected = dot_nt(weights[: 2 * CH, :], normed)
                turned[pl.ds(i, CH, stride=8), :] = (jnp.tanh(projected[CH:]) + 1.0) * projected[:CH]
                turned[pl.ds(8 * CH + i, ROW, stride=8), :] = dot_nt(weights[4 * CH :, :], normed)
            left_s[:, first + b] = turned[: 8 * CH].reshape(CH, 8, BLK).astype(BF16)
            bias_s[:, first + b] = turned[8 * CH :].reshape(ROW, 8, BLK).astype(BF16)

    start(bias_c)
    for q in range(QC):
        start(left_c[q])

    @pl.when(fetches)
    def _():
        start(wo_c + [wo_own])

    exchange_channel(1)

    for h, (first, count) in enumerate(PARTS):

        @pl.loop(0, count)
        def _(b):
            values = pair_v[h][b].reshape(8 * BLK, CZ)
            shifted[...] = values.astype(F32) - dot_nn(values, ones[...])
            squares = (shifted[...] * shifted[...]).astype(BF16)
            for i in range(8):
                spread = dot_nt(ones[:8], squares[i * BLK : (i + 1) * BLK])
                scale_out[first + b, i : i + 1, :] = lax.rsqrt(spread[:1] + EPS)
            inverse[...] = jnp.tanh(dot_nn(normed_v[h][b], gates[...])) + 1.0
            pair_v[h][b] = inverse[...].astype(BF16).reshape(8, BLK, CZ)

        saves.append(pltpu.make_async_copy(pair_v[h], gate_out.at[pl.ds(first, count)], save_s.at[1, h]))
        saves[-1].start()

    exchange_channel(2)
    exchange_channel(3)

    @pl.loop(0, NB)
    def _(b):
        write_places(cols, grp, b, place, kvplace)

    for c in kv_c:
        c.wait()
    for c in bias_c:
        c.wait()
    kv_all[:BR] = kv_own[...]
    kv_all[BR:] = kv_r[...]
    chain_bias = same[row]

    @pl.loop(0, BR)
    def _(r):
        here = chain[grp * BR + r]
        query = queries[r]
        cot = cots[r]
        top = jnp.full((BLK, 1), -jnp.inf, F32)
        for s in range(KS):
            kv = kv_all[kvplace[r * KS + s]]
            j = cols[s, grp * BR + r]
            extra = jnp.where(chain[j] == here, chain_bias, 0.0)
            part = dot_nt(query, kv) * (48 ** -0.5) + (bias[r * KS + s].astype(F32) + extra)
            part = jnp.where(mask[s, grp * BR + r] > 0, part, -jnp.inf)
            scores[s] = part
            gprobs[s] = dot_nt(cot, kv)
            top = jnp.maximum(top, jnp.max(part, axis=1, keepdims=True))
        total = jnp.zeros((BLK, 1), F32)
        for s in range(KS):
            part = jnp.exp(scores[s] - top)
            scores[s] = part
            total = total + jnp.sum(part, axis=1, keepdims=True)
        inverse = 1.0 / total
        dots = jnp.zeros((BLK, 1), F32)
        mix = jnp.zeros((BLK, PAD), F32)
        for s in range(KS):
            probs = scores[s] * inverse
            scores[s] = probs
            dots = dots + jnp.sum(probs * gprobs[s], axis=1, keepdims=True)
            mix = mix + dot_nn(probs.astype(BF16), kv_all[kvplace[r * KS + s]])
        for s in range(KS):
            grads[r * KS + s] = (scores[s] * (gprobs[s] - dots)).astype(BF16)
        mixed[pl.ds(pl.multiple_of(r * BLK, BLK), BLK), :] = mix.astype(BF16)

    slot = lambda p: pl.ds(pl.multiple_of(p * 8, 8), 8)
    rows32 = lambda p: pl.ds(pl.multiple_of(p * 32, 32), 32)
    mix_c = [
        to_row(mixed.at[rows32(p)], mixed_r.at[row], mix_ss.at[n], mix_rs.at[n], p) for n, p in enumerate(peers)
    ]
    mix_own = pltpu.make_async_copy(mixed.at[rows32(row)], mixed_r.at[row], own_s.at[0, 2 * QC + 2])
    grad_c = [
        to_row(grads.at[:, slot(p), :], grad_out.at[:, row], grad_ss.at[n], grad_rs.at[n], p)
        for n, p in enumerate(peers)
    ]
    grad_own = pltpu.make_async_copy(grads.at[:, mine, :], grad_out.at[:, row], own_s.at[0, 2 * QC + 3])
    for c in mix_c + [mix_own] + grad_c + [grad_own]:
        c.start()

    tri_c = []
    wx_c = [
        to_grp(wo_all.at[:, :, sixth], wo_all.at[:, :, sixth], wx_ss.at[n], wx_rs.at[n], gpeers[n])
        for n in range(7)
    ]
    for q in range(QC):
        if q == QC - 1:

            @pl.when(fetches)
            def _():
                for c in wo_c + [wo_own]:
                    c.wait()
                for c in wx_c:
                    c.start()

        for c in left_c[q]:
            c.wait()
        for c in x_c[q]:
            c.wait()

        cuts = ((0, NB),) if q < QC - 1 else ((0, NB // 2), (NB // 2, NB // 2))
        for h, (first, count) in enumerate(cuts):

            @pl.loop(first, first + count)
            def _(b):
                r = b // KS
                lhs, rhs = [], []
                for t in range(KS):
                    code = place[b * KS + t]
                    near = right[q][jnp.minimum(code, NB - 1)]
                    far = xr[q][jnp.clip(code - NB, 0, 55)]
                    block = jnp.where(code < NB, near, far)
                    rhs.append(jnp.where(code < NB + 56, block, jnp.zeros_like(block)))
                    lhs.append(left[q][r * KS + t])
                tri[q][b] = dot_nt(jnp.concatenate(lhs, axis=1), jnp.concatenate(rhs, axis=1)).astype(BF16)

            here = pl.ds(first, count)
            tri_c.append([
                to_row(tri[q].at[here, slot(p), :], tri_out.at[here, q, row], tri_ss.at[q + h, n], tri_rs.at[q + h, n], p)
                for n, p in enumerate(peers)
            ] + [pltpu.make_async_copy(tri[q].at[here, mine, :], tri_out.at[here, q, row], own_s.at[1, 8 + q + h])])
            start(tri_c[-1])

    for c in mix_c + [mix_own]:
        c.wait()

    @pl.when(fetches)
    def _():
        for c in wx_c:
            c.wait_send()

    for n, o in enumerate(GRP_ORDER):

        @pl.when((chip - o // 2 + 4) % 4 < 3)
        def _():
            wx_c[n].wait_recv()

    acc = nodes[rows32(row), :].astype(F32)
    for p in range(ROW):
        acc = acc + dot_nn(mixed_r[p, :, VOFF : VOFF + 48], wo_all[p])
    node_out[...] = acc.astype(BF16)

    for c in saves + grad_c + [grad_own]:
        c.wait()
    for part in tri_c:
        for c in part:
            c.wait()


def exchange(scalars, tensors, nodes):
    smem = pl.BlockSpec(memory_space=pltpu.SMEM)
    vmem = pl.BlockSpec(memory_space=pltpu.VMEM)
    anyspace = pl.BlockSpec(memory_space=pl.ANY)
    dma = pltpu.SemaphoreType.DMA
    blocks = lambda n: pltpu.VMEM((n, BLK, BLK), BF16)
    blocks_2d = pltpu.VMEM((BLK, BLK), BF16)
    n = ROW - 1
    scratch = (
        [blocks(NB)] * QC + [blocks(NB)] * QC + [blocks(NB)] * QC + [blocks(56)] * QC + [blocks(56)] * QC
        + [pltpu.VMEM((ROW, k, 8, BLK), BF16) for _, k in PARTS]
        + [pltpu.VMEM((CH - ROW, k, 8, BLK), BF16) for _, k in PARTS]
        + [pltpu.VMEM((CH, NB, 8, BLK), BF16), pltpu.VMEM((ROW, NB, 8, BLK), BF16)]
        + [pltpu.VMEM((k, 8, BLK, CZ), BF16) for _, k in PARTS]
        + [pltpu.VMEM((k, 8 * BLK, CZ), BF16) for _, k in PARTS]
        + [
            pltpu.VMEM((4 * CH + ROW, CZ), BF16), blocks_2d, pltpu.VMEM(((CH + ROW) * 8, BLK), F32),
            pltpu.VMEM((8 * BLK, CZ), F32), pltpu.VMEM((8 * BLK, CZ), F32), blocks_2d,
            pltpu.VMEM((2 * ROW, CZ), BF16), pltpu.VMEM((2 * (CH - ROW), CZ), BF16),
            pltpu.SMEM((NB * KS,), jnp.int32), pltpu.SMEM((NB,), jnp.int32),
            pltpu.SMEM((56,), jnp.int32), pltpu.SMEM((14,), jnp.int32),
        ]
        + [
            blocks(NB), blocks(NB), blocks(BR), blocks(14), blocks(14), blocks(BR + 14), blocks(BR), blocks(BR),
            pltpu.VMEM((BR * BLK, PAD), BF16), pltpu.VMEM((ROW, 32, PAD), BF16),
            pltpu.VMEM((ROW, 48, 768), BF16), pltpu.VMEM((PAD, 768), BF16), pltpu.VMEM((PAD, 768), BF16),
            pltpu.VMEM((PAD, 768), BF16), pltpu.VMEM((KS, BLK, BLK), F32), pltpu.VMEM((KS, BLK, BLK), F32),
        ]
        + [dma((len(PARTS) * QC, n))] * 2 + [dma((QC, n))] * 2 + [dma((QC + 1, n))] * 2 + [dma((QC, 7))] * 2 + [dma((7,))] * 2 + [dma((n,))] * 8
        + [dma((len(PARTS), 2 * QC + 1 + QC)), dma((len(PARTS),)), dma((7,)), dma((7,)), dma((2, len(PARTS)))]
    )
    return pl.pallas_call(
        exchange_kernel,
        in_specs=[smem] * 4 + [anyspace] + [vmem] * 9,
        out_specs=[anyspace, anyspace, vmem, anyspace, anyspace, vmem],
        out_shape=[
            jax.ShapeDtypeStruct((NB, QC, ROW, 8, BLK), BF16),
            jax.ShapeDtypeStruct((NB, ROW, 8, BLK), BF16),
            jax.ShapeDtypeStruct((32, 768), BF16),
            jax.ShapeDtypeStruct((NB, 8 * BLK, CZ), BF16),
            jax.ShapeDtypeStruct((NB, 8, BLK, CZ), BF16),
            jax.ShapeDtypeStruct((NB, 8, BLK), F32),
        ],
        scratch_shapes=scratch,
        compiler_params=pltpu.CompilerParams(
            collective_id=0, has_side_effects=True, vmem_limit_bytes=63<<20
        ),
        name="exchange",
    )(*scalars, *tensors, *nodes)


def finish_kernel(
    pair, tri, grads, normed, gate, scale, out_w, bias_w, pair_out, pair_grad,
    weights, ones, turned, hidden, both, along,
):
    @pl.when(pl.program_id(0) == 0)
    def _():
        bias = bias_w[...].astype(F32)
        weights[...] = jnp.zeros_like(weights)
        weights[:CH, :CZ] = out_w[...] * 0.5
        weights[CH : CH + ROW, CZ:] = (bias - jnp.mean(bias, axis=1, keepdims=True)).astype(BF16)
        ones[...] = jnp.full_like(ones, 1.0 / CZ)
        turned[...] = jnp.zeros_like(turned)

    def norm(k):
        sums = tri[k].astype(F32)
        centred = sums - jnp.mean(sums, axis=0, keepdims=True)
        spread = jnp.mean(centred * centred, axis=0, keepdims=True)
        turned[k, : 8 * CH] = (centred * lax.rsqrt(spread + EPS)).reshape(8 * CH, BLK)
        turned[k, 8 * CH : 8 * (CH + ROW)] = (grads[k].astype(F32) * scale[k]).reshape(8 * ROW, BLK)

    def turn(k):
        for i in range(8):
            hidden[k, i * BLK : (i + 1) * BLK, :] = turned[k, pl.ds(i, PAD, stride=8), :].astype(BF16).T

    def product(k):
        both[k] = dot_nn(hidden[k], weights[...])

    def project(k):
        along[k] = dot_nn(both[k, :, CZ:].astype(BF16) * normed[k], ones[...])

    def store(k):
        for i in range(8):
            rows = slice(i * BLK, (i + 1) * BLK)
            pair_out[k, i] = pair[k, i] + gate[k, i] * both[k, rows, :CZ].astype(BF16)
            pair_grad[k, i] = both[k, rows, CZ:].astype(BF16) - normed[k, rows, :] * along[k, rows, :].astype(BF16)

    norm(0)
    for k in range(STEP):
        turn(k)
        if k + 1 < STEP:
            norm(k + 1)
        product(k)
        if k > 0:
            store(k - 1)
        project(k)
    store(STEP - 1)


def finish(pair, tri, grads, normed, gate, scale, out_w, bias_w):
    by_block = lambda a: pl.BlockSpec((STEP,) + a.shape[1:], lambda b: (b,) + (0,) * (a.ndim - 1))
    whole = lambda a: pl.BlockSpec(a.shape, lambda b: (0,) * a.ndim)
    return pl.pallas_call(
        finish_kernel,
        grid=(NB // STEP,),
        in_specs=[by_block(a) for a in (pair, tri, grads, normed, gate, scale)] + [whole(out_w), whole(bias_w)],
        out_specs=[by_block(pair), by_block(pair)],
        out_shape=[jax.ShapeDtypeStruct(pair.shape, BF16)] * 2,
        scratch_shapes=[
            pltpu.VMEM((PAD, 2 * CZ), BF16),
            pltpu.VMEM((CZ, CZ), BF16),
            pltpu.VMEM((STEP, PAD * 8, BLK), F32),
            pltpu.VMEM((STEP, 8 * BLK, PAD), BF16),
            pltpu.VMEM((STEP, 8 * BLK, 2 * CZ), F32),
            pltpu.VMEM((STEP, 8 * BLK, CZ), F32),
        ],
        compiler_params=pltpu.CompilerParams(vmem_limit_bytes=62<<20),
        name="finish",
    )(pair, tri, grads, normed, gate, scale, out_w, bias_w)


def per_device(
    pair_feats,
    block_cols,
    attn_mask,
    chain_of_row,
    same_chain,
    node_feats,
    node_cotangent,
    tri_weight,
    gate_weight,
    tri_out_weight,
    bias_weight,
    query_weight,
    key_weight,
    value_weight,
    out_weight,
):
    pair = pair_feats.reshape(NB, 8, BLK, CZ)
    bias_t = bias_weight.T
    tri, grads, node_out, normed, gate, scale = exchange(
        (block_cols.T, attn_mask.T, chain_of_row, same_chain),
        (pair, tri_weight, gate_weight, bias_t),
        (node_feats, node_cotangent, query_weight.T, key_weight.T, value_weight.T, out_weight),
    )
    pair_out, pair_grad = finish(
        pair, tri.reshape(NB, CH, 8, BLK), grads, normed, gate, scale, tri_out_weight, bias_t
    )
    return pair_out.reshape(pair_feats.shape), node_out, pair_grad.reshape(pair_feats.shape)


def solution(mesh):
    pair_spec = P("grp", None, "row", None, None)
    node_spec = P("grp", None)
    in_specs = (
        (pair_spec,) + (P(),) * 4 + (node_spec,) * 2 + (P(),) * 4 + (P(None, "row"),) * 3 + (P("row", None),)
    )
    out_specs = (pair_spec, P(("grp", "row"), None), pair_spec)
    return jax.shard_map(per_device, mesh=mesh, in_specs=in_specs, out_specs=out_specs, check_vma=False)
```
